512 devices in a mesh: row: 16 (over y, core), col: 32 (over z, x).
Axes of the slice: x: 4, y: 8, z: 8, core: 2. Of those that a mesh axis runs over, the one named last changes fastest.
Arguments:
- surface: float32 [2, 1024, 4096], P(None, 'row', 'col'), may hold values from -0.5 to 0.5
- u_face: float32 [2, 1024, 4096], P(None, 'row', 'col'), may hold values from -3 to 3
- v_face: float32 [2, 1024, 4096], P(None, 'row', 'col'), may hold values from -3 to 3
- bed_depth: float32 [1024, 4096], P('row', 'col'), may hold values from 1 to 10
- wet_mask: int32 [2, 1024, 4096], P(None, 'row', 'col'), may hold values 0 or 1
- rainfall: float32 [2, 1024, 4096], P(None, 'row', 'col'), may hold values from 0.05 to 0.5
Outputs:
- new_surface: float32 [2, 1024, 4096], P(None, 'row', 'col')
- new_u: float32 [2, 1024, 4096], P(None, 'row', 'col')
- new_v: float32 [2, 1024, 4096], P(None, 'row', 'col')
The draws below stay inside these ranges and needn't reach their ends.
All inputs are finite; a program needn't handle non-finite values. No bound on the sum of `wet_mask` on one device may be relied on, other than what follows from the above.
Results may differ from the reference program's by a relative error of at most 0.0003.
Values sent between devices are 32-bit elements; how exact they have to be, the bound alone decides.
A program may use at most 64 MiB of HBM per device.

```python
import math
import jax
import jax.numpy as jnp

M = 2
ITERS = 3
NY = 1024
NX = 4096


def touch_ends(drawn, key, smallest, top_value):
    place = [jax.random.randint(jax.random.fold_in(key, axis), (), 0, length) for axis, length in enumerate(drawn.shape)]
    longest = drawn.shape.index(max(drawn.shape))
    neighbour = place[:longest] + [(place[longest] + 1) % drawn.shape[longest]] + place[longest + 1:]
    return drawn.at[tuple(place)].set(smallest).at[tuple(neighbour)].set(top_value)


def steps_of(own_key, shape, cuts, low, high):
    factor_of, own = 1.0, jax.random.fold_in(own_key, 6)
    for position, shards_of in cuts:
        heights = jnp.exp(jax.random.uniform(jax.random.fold_in(own, position), (shards_of,), jnp.float32, low / len(cuts), high / len(cuts)))
        factor_of = factor_of * jnp.repeat(heights, shape[position] // shards_of).reshape([-1 if axis == position else 1 for axis in range(len(shape))])
    return factor_of


def normal_values(own_key, extent, deviation, most, split=(), held_as=jnp.bfloat16):
    level = steps_of(own_key, extent, split, -0.22, 0.18) if split else 1.0
    result = jax.random.normal(own_key, extent, jnp.float32) * deviation * level
    return jnp.minimum(jnp.maximum(result, -most), most).astype(held_as)


def setup_inputs(seed: int = 0) -> dict:
    arg_keys = jax.random.split(jax.random.key(seed), 7)
    return {
        "surface": jnp.clip(jax.random.uniform(arg_keys[0], (M, NY, NX), jnp.float32, -0.5, 0.5) * steps_of(arg_keys[0], (M, NY, NX), ((1, 16), (2, 32)), -0.4, 0.0), -0.5, 0.5),
        "u_face": normal_values(arg_keys[1], (M, NY, NX), 0.5, 3.0, ((1, 16), (2, 32)), jnp.float32),
        "v_face": normal_values(arg_keys[2], (M, NY, NX), 0.5, 3.0, ((1, 16), (2, 32)), jnp.float32),
        "bed_depth": jnp.clip(jnp.exp(math.log(10.0) - 2.3025851 * jax.random.uniform(arg_keys[3], (NY, NX), jnp.float32) ** steps_of(arg_keys[3], (NY, NX), ((0, 16), (1, 32)), -0.2, 0.2)), 1.0, 10.0),
        "wet_mask": touch_ends((jax.random.randint(arg_keys[4], (M, NY, NX), 0, 8) < 7).astype(jnp.int32), jax.random.fold_in(arg_keys[4], 1), 0, 1),
        "rainfall": jnp.clip(jnp.exp(math.log(0.5) - 2.3025851 * jax.random.uniform(arg_keys[5], (M, NY, NX), jnp.float32) ** steps_of(arg_keys[5], (M, NY, NX), ((1, 16), (2, 32)), -0.2, 0.2)), 0.05, 0.5),
    }


DTDX = 0.5
FRIC = 0.05
G1 = 4.0
CK = DTDX * G1


def explicit(eta2, u2, v2, dep2, wet2, ny, nx):
    def view(a, dy, dx):
        return a[:, 1 + dy:3 + dy + ny, 1 + dx:3 + dx + nx]
    h_here = view(eta2, 0, 0) + view(dep2, 0, 0)
    h_east = view(eta2, 0, 1) + view(dep2, 0, 1)
    h_north = view(eta2, 1, 0) + view(dep2, 1, 0)
    wet_x = view(wet2, 0, 0) * view(wet2, 0, 1)
    wet_y = view(wet2, 0, 0) * view(wet2, 1, 0)
    depth_x = 0.5 * (h_here + h_east)
    depth_y = 0.5 * (h_here + h_north)
    u_here = view(u2, 0, 0)
    v_here = view(v2, 0, 0)
    v_mean = 0.25 * (v_here + view(v2, 0, 1) + view(v2, -1, 0) + view(v2, -1, 1))
    u_mean = 0.25 * (u_here + view(u2, 0, -1) + view(u2, 1, 0) + view(u2, 1, -1))
    adv_u = jnp.where(u_here > 0, u_here * (u_here - view(u2, 0, -1)), u_here * (view(u2, 0, 1) - u_here))
    adv_u = adv_u + jnp.where(v_mean > 0, v_mean * (u_here - view(u2, -1, 0)), v_mean * (view(u2, 1, 0) - u_here))
    adv_v = jnp.where(v_here > 0, v_here * (v_here - view(v2, -1, 0)), v_here * (view(v2, 1, 0) - v_here))
    adv_v = adv_v + jnp.where(u_mean > 0, u_mean * (v_here - view(v2, 0, -1)), u_mean * (view(v2, 0, 1) - v_here))
    u_star = wet_x * (u_here - DTDX * adv_u) / (1.0 + FRIC * jnp.abs(u_here))
    v_star = wet_y * (v_here - DTDX * adv_v) / (1.0 + FRIC * jnp.abs(v_here))
    return u_star, v_star, wet_x, wet_y, CK * depth_x * wet_x, CK * depth_y * wet_y, depth_x * u_star, depth_y * v_star


def inner(a):
    return a[:, 1:-1, 1:-1]


def right_side(eta, rain, flux_x, flux_y):
    div = (inner(flux_x) - flux_x[:, 1:-1, :-2]) + (inner(flux_y) - flux_y[:, :-2, 1:-1])
    return eta + rain - DTDX * div


def operate(e_pad, coef_x, coef_y):
    e_mid = inner(e_pad)
    out = e_mid + inner(coef_x) * (e_mid - e_pad[:, 1:-1, 2:]) + coef_x[:, 1:-1, :-2] * (e_mid - e_pad[:, 1:-1, :-2])
    return out + inner(coef_y) * (e_mid - e_pad[:, 2:, 1:-1]) + coef_y[:, :-2, 1:-1] * (e_mid - e_pad[:, :-2, 1:-1])


def pad_one(a):
    return jnp.pad(a, ((0, 0), (1, 1), (1, 1)))


def reference(surface, u_face, v_face, bed_depth, wet_mask, rainfall):
    ny = surface.shape[1]
    nx = surface.shape[2]
    widths = ((0, 0), (2, 2), (2, 2))
    eta2 = jnp.pad(surface, widths)
    u2 = jnp.pad(u_face, widths)
    v2 = jnp.pad(v_face, widths)
    dep2 = jnp.pad(bed_depth[None], widths)
    wet2 = jnp.pad(wet_mask.astype(jnp.float32), widths)
    u_star, v_star, wet_x, wet_y, coef_x, coef_y, flux_x, flux_y = explicit(eta2, u2, v2, dep2, wet2, ny, nx)
    rhs = right_side(surface, rainfall, flux_x, flux_y)
    solution = surface
    residual = rhs - operate(pad_one(surface), coef_x, coef_y)
    direction = residual
    norm_now = jnp.sum(residual * residual, axis=(1, 2))
    for step in range(ITERS):
        image = operate(pad_one(direction), coef_x, coef_y)
        alpha = norm_now / jnp.sum(direction * image, axis=(1, 2))
        solution = solution + alpha[:, None, None] * direction
        residual = residual - alpha[:, None, None] * image
        norm_next = jnp.sum(residual * residual, axis=(1, 2))
        direction = residual + (norm_next / norm_now)[:, None, None] * direction
        norm_now = norm_next
    full = pad_one(solution)
    new_u = inner(u_star) - G1 * inner(wet_x) * (full[:, 1:-1, 2:] - solution)
    new_v = inner(v_star) - G1 * inner(wet_y) * (full[:, 2:, 1:-1] - solution)
    return solution, new_u, new_v
```

```python
import functools

import jax
import jax.numpy as jnp
from jax import lax
from jax.experimental import pallas as pl
from jax.experimental.pallas import tpu as pltpu
from jax.sharding import PartitionSpec as P

DTDX = 0.5
FRIC = 0.05
G1 = 4.0
CK = DTDX * G1
MESH = pl.DeviceIdType.MESH
F32 = jnp.float32

SURF, UF, VF, RAIN, WET, DEP = range(6)
SHIFT = (0, 8, 16, 48, 56, 64)
PLANES = tuple((f, m) for f in range(6) for m in range(2))
ROWS = 64
TOP = 8
TALL = 80
SIDES = ((1, 0), (-1, 0), (0, 1), (0, -1), (1, 1), (1, -1), (-1, 1), (-1, -1))


def lanes(shape):
    return lax.broadcasted_iota(jnp.int32, shape, len(shape) - 1)


def turn(x, amount):
    return pltpu.roll(x, amount % 128, x.ndim - 1)


def kernel(nrow, ncol, surf_h, u_h, v_h, bed_h, wet_h, rain_h, x_o, nu_o, nv_o,
           field, weti, own_seam, pack_n, pack_s, pack_c, got_n, got_s, got_e, got_w,
           fluxy, kx, ky, wx4, wy4, ub, vb, basis, dxs, dys, out,
           tile1, tile2, tile3, in_sem, out_sem, send_sem, recv_sem, sum_send, sum_recv):
    r0 = lax.axis_index("row")
    c0 = lax.axis_index("col")
    y, core = r0 // 2, r0 % 2
    z, x = c0 // 4, c0 % 4
    q = x * 2 + core

    loads = [
        pltpu.make_async_copy(surf_h, field.at[SURF, 0:2, TOP:TOP + ROWS, :], in_sem.at[0]),
        pltpu.make_async_copy(u_h, field.at[UF, 0:2, TOP:TOP + ROWS, :], in_sem.at[1]),
        pltpu.make_async_copy(v_h, field.at[VF, 0:2, TOP:TOP + ROWS, :], in_sem.at[2]),
        pltpu.make_async_copy(bed_h, field.at[DEP, 0, TOP:TOP + ROWS, :], in_sem.at[3]),
        pltpu.make_async_copy(bed_h, field.at[DEP, 1, TOP:TOP + ROWS, :], in_sem.at[4]),
        pltpu.make_async_copy(wet_h, weti, in_sem.at[5]),
        pltpu.make_async_copy(rain_h, field.at[RAIN, 0:2, TOP:TOP + ROWS, :], in_sem.at[6]),
    ]
    for load in loads:
        load.start()

    def exists(dr, dc):
        ok = None
        for here, step, count in ((r0, dr, nrow), (c0, dc, ncol)):
            if step:
                there = (here + step >= 0) & (here + step < count)
                ok = there if ok is None else ok & there
        return ok

    barrier = pltpu.get_barrier_semaphore()
    groups = [
        [(r0, 4 * ((z + d) % 8) + x) for d in range(1, 8)],
        [(2 * ((y + d) % 8) + core, c0) for d in range(1, 8)],
        [(2 * y + (q + d) % 2, 4 * z + ((q + d) % 8) // 2) for d in range(1, 8)],
    ]
    places = [z, y, q]
    for dr, dc in SIDES:
        @pl.when(exists(dr, dc))
        def _():
            pl.semaphore_signal(barrier, inc=1, device_id=(r0 + dr, c0 + dc), device_id_type=MESH)
    for group in groups:
        for partner in group:
            pl.semaphore_signal(barrier, inc=1, device_id=partner, device_id_type=MESH)

    zero = lambda ref, a, b: ref.__setitem__((slice(a, b), slice(None)), jnp.zeros((b - a, 128), F32))
    for (dr, dc), ref, a, b in (
        ((1, 0), got_n, 0, 48), ((-1, 0), got_s, 0, 48),
        ((0, 1), got_e, 8, 72), ((0, -1), got_w, 8, 72),
        ((1, 1), got_e, 72, 80), ((-1, 1), got_e, 0, 8),
        ((1, -1), got_w, 72, 80), ((-1, -1), got_w, 0, 8),
    ):
        @pl.when(jnp.logical_not(exists(dr, dc)))
        def _():
            zero(ref, a, b)

    for load in loads:
        load.wait()
    for m in range(2):
        field[WET, m, TOP:TOP + ROWS, :] = weti[m].astype(F32)

    for p, (f, m) in enumerate(PLANES):
        pack_n[4 * p:4 * p + 4, :] = field[f, m, TOP + ROWS - 4:TOP + ROWS, :]
        pack_s[4 * p:4 * p + 4, :] = field[f, m, TOP:TOP + 4, :]

    def pack_columns(c, carry):
        row = pl.multiple_of(c * 8, 8)
        lane = lanes((8, 128))
        acc = jnp.zeros((8, 128), F32)
        for f, m in PLANES:
            base = SHIFT[f] + 8 + 24 * m
            rolled = turn(field[f, m, pl.ds(TOP + row, 8), :], base + 4)
            acc = jnp.where((lane >= base) & (lane < base + 8), rolled, acc)
        pack_c[pl.ds(row, 8), :] = acc
        return carry

    lax.fori_loop(0, 8, pack_columns, 0)

    north, south = (r0 + 1 < nrow).astype(jnp.int32), (r0 > 0).astype(jnp.int32)
    east, west = (c0 + 1 < ncol).astype(jnp.int32), (c0 > 0).astype(jnp.int32)
    peers = 21 + (1 + north + south) * (1 + east + west) - 1
    pl.semaphore_wait(barrier, peers)

    def halo(k):
        dr, dc = SIDES[k]
        if dc == 0:
            src, dst = (pack_n, got_s) if dr == 1 else (pack_s, got_n)
        else:
            lands = got_w if dc == 1 else got_e
            if dr == 0:
                src, dst = pack_c, lands.at[8:72, :]
            elif dr == 1:
                src, dst = pack_c.at[56:64, :], lands.at[0:8, :]
            else:
                src, dst = pack_c.at[0:8, :], lands.at[72:80, :]
        return pltpu.make_async_remote_copy(
            src_ref=src, dst_ref=dst, send_sem=send_sem.at[k], recv_sem=recv_sem.at[k],
            device_id=(r0 + dr, c0 + dc), device_id_type=MESH)

    for k, (dr, dc) in enumerate(SIDES):
        @pl.when(exists(dr, dc))
        def _():
            halo(k).start()

    def seam_own(row):
        lane = lanes((8, 128))
        for f in range(6):
            a = field[f, 0, pl.ds(row, 8), :]
            b = field[f, 1, pl.ds(row, 8), :]
            m0 = jnp.where(lane < 12, turn(a, 8), turn(a, 16))
            m1 = jnp.where(lane < 36, turn(b, 32), turn(b, 40))
            own_seam[f, pl.ds(row, 8), :] = jnp.where(lane < 24, m0, m1)

    def seam_body(c, carry):
        seam_own(pl.multiple_of(c * 8 + 8, 8))
        return carry

    lax.fori_loop(0, 8, seam_body, 0)

    for k, (dr, dc) in enumerate(SIDES):
        @pl.when(exists(-dr, -dc))
        def _():
            halo(k).wait_recv()

    for p, (f, m) in enumerate(PLANES):
        field[f, m, 72:76, :] = got_n[4 * p:4 * p + 4, :]
        field[f, m, 4:8, :] = got_s[4 * p:4 * p + 4, :]
    seam_own(0)
    seam_own(72)

    def seam_halo(c, carry):
        row = pl.multiple_of(c * 8, 8)
        lane = lanes((8, 128))
        both = jnp.where((lane & 4) == 0, turn(got_e[pl.ds(row, 8), :], -4), turn(got_w[pl.ds(row, 8), :], 4))
        ghost = ((lane >= 8) & (lane < 16)) | ((lane >= 32) & (lane < 40))
        for f in range(6):
            field[f, 2, pl.ds(row, 8), :] = jnp.where(ghost, turn(both, -SHIFT[f]), own_seam[f, pl.ds(row, 8), :])
        return carry

    lax.fori_loop(0, 10, seam_halo, 0)

    def first(c, carry):
        row = 5 + c * 8

        def at(f, d):
            return field[f, :, pl.ds(row + d, 8), :]

        eta = at(SURF, 0)
        eta_n = at(SURF, 1)
        h = eta + at(DEP, 0)
        h_n = eta_n + at(DEP, 1)
        wet = at(WET, 0)
        u, u_n, u_s = at(UF, 0), at(UF, 1), at(UF, -1)
        v, v_n, v_s = at(VF, 0), at(VF, 1), at(VF, -1)
        wet_x = wet * turn(wet, -1)
        wet_y = wet * at(WET, 1)
        hx = 0.5 * (h + turn(h, -1))
        hy = 0.5 * (h + h_n)
        vs = v + v_s
        vbar = 0.25 * (vs + turn(vs, -1))
        us = u + u_n
        ubar = 0.25 * (us + turn(us, 1))
        adv_u = u * jnp.where(u > 0, u - turn(u, 1), turn(u, -1) - u)
        adv_u = adv_u + vbar * jnp.where(vbar > 0, u - u_s, u_n - u)
        adv_v = v * jnp.where(v > 0, v - v_s, v_n - v)
        adv_v = adv_v + ubar * jnp.where(ubar > 0, v - turn(v, 1), turn(v, -1) - v)
        u_star = wet_x * (u - DTDX * adv_u) / (1.0 + FRIC * jnp.abs(u))
        v_star = wet_y * (v - DTDX * adv_v) / (1.0 + FRIC * jnp.abs(v))
        kx_c = CK * hx * wet_x
        ky_c = CK * hy * wet_y
        drop_x = eta - turn(eta, -1)
        drop_y = eta - eta_n
        fx = DTDX * (hx * u_star) + kx_c * drop_x
        fy = DTDX * (hy * v_star) + ky_c * drop_y
        fluxy[:, pl.ds(row, 8), :] = fy
        kx[:, pl.ds(row, 8), :] = kx_c
        ky[:, pl.ds(row, 8), :] = ky_c
        wx4[:, pl.ds(row, 8), :] = G1 * wet_x
        wy4[:, pl.ds(row, 8), :] = G1 * wet_y
        ub[:, pl.ds(row, 8), :] = u_star + G1 * wet_x * drop_x
        vb[:, pl.ds(row, 8), :] = v_star + G1 * wet_y * drop_y
        basis[0, :, pl.ds(row, 8), :] = (
            at(RAIN, 0) - (fx - turn(fx, 1)) - (fy - fluxy[:, pl.ds(row - 1, 8), :]))
        return carry

    lax.fori_loop(0, 9, first, 0)

    def apply(k, start):
        def body(c, carry):
            row = start + c * 8
            here = pl.ds(row, 8)
            below = pl.ds(row - 1, 8)
            e = basis[k, :, here, :]
            gx = kx[:, here, :] * (e - turn(e, -1))
            gy = ky[:, here, :] * (e - basis[k, :, pl.ds(row + 1, 8), :])
            gs = ky[:, below, :] * (basis[k, :, below, :] - e)
            basis[k + 1, :, here, :] = gx - turn(gx, 1) + (gy - gs)
            return carry

        lax.fori_loop(0, 9, body, 0)

    apply(0, 7)
    apply(1, 8)

    def sums(c, acc):
        row = pl.multiple_of(8 + c * 8, 8)
        here = pl.ds(row, 8)
        v0 = basis[0, :, here, :]
        v1 = basis[1, :, here, :]
        v2 = basis[2, :, here, :]
        dx = turn(v2, -1) - v2
        dy = basis[2, :, pl.ds(row + 1, 8), :] - v2
        terms = (v0 * v0, v0 * v1, v1 * v1, v1 * v2, v2 * v2,
                 kx[:, here, :] * (dx * dx) + ky[:, here, :] * (dy * dy))
        return tuple(a + t for a, t in zip(acc, terms))

    acc = lax.fori_loop(0, 8, sums, tuple(jnp.zeros((3, 8, 128), F32) for _ in range(6)))
    lane = lanes((8, 128))
    sub = lax.broadcasted_iota(jnp.int32, (8, 128), 0)
    own_ok = (lane >= 4) & (lane < 124)
    seam_ok = [((lane >= 4 + 24 * m) & (lane < 8 + 24 * m)) | ((lane >= 16 + 24 * m) & (lane < 20 + 24 * m))
               for m in range(2)]
    rows = []
    for m in range(2):
        table = jnp.zeros((8, 128), F32)
        for k in range(6):
            part = jnp.where(own_ok, acc[k][m], 0.0) + jnp.where(seam_ok[m], acc[k][2], 0.0)
            total = jnp.sum(part, axis=0, keepdims=True)
            table = jnp.where(sub == k, total, table)
        rows.append(table)
    even = (lane & 1) == 0
    tile = jnp.where(even, rows[0] + turn(rows[0], -1), rows[1] + turn(rows[1], 1))
    for amount in (2, 4, 8, 16, 32, 64):
        tile = tile + turn(tile, amount)

    def send_tile(s, slots, value):
        slots[places[s]] = value
        for d in range(7):
            pltpu.make_async_remote_copy(
                src_ref=slots.at[places[s]], dst_ref=slots.at[places[s]],
                send_sem=sum_send.at[s, d], recv_sem=sum_recv.at[s],
                device_id=groups[s][d], device_id_type=MESH).start()

    def take_tiles(s, slots):
        pltpu.make_async_copy(slots.at[0:7], slots.at[0:7], sum_recv.at[s]).wait()
        total = slots[0]
        for k in range(1, 8):
            total = total + slots[k]
        return total

    send_tile(0, tile1, tile)

    def join(c, carry):
        row = pl.multiple_of(8 + c * 8, 8)
        here = pl.ds(row, 8)
        lane = lanes((8, 128))

        def merged(block):
            full = []
            for m in range(2):
                west = turn(block[2], -16 - 24 * m)
                east = turn(block[2], 120 - 24 * m)
                full.append(jnp.where(lane < 4, west, jnp.where(lane >= 124, east, block[m])))
            return full

        wx_c = wx4[:, here, :]
        wy_c = wy4[:, here, :]
        for k in range(3):
            e = basis[k, :, here, :]
            e_n = basis[k, :, pl.ds(row + 1, 8), :]
            for m, value in enumerate(merged(wx_c * (turn(e, -1) - e))):
                dxs[k, m, pl.ds(row - 8, 8), :] = value
            for m, value in enumerate(merged(wy_c * (e_n - e))):
                dys[k, m, pl.ds(row - 8, 8), :] = value
            west_east = merged(e)
            for m in range(2):
                basis[k, m, here, :] = west_east[m]
        for ref, slot in ((ub, 1), (vb, 2)):
            for m, value in enumerate(merged(ref[:, here, :])):
                out[slot, m, pl.ds(row - 8, 8), :] = value
        return carry

    lax.fori_loop(0, 8, join, 0)

    send_tile(1, tile2, take_tiles(0, tile1))
    send_tile(2, tile3, take_tiles(1, tile2))
    total = take_tiles(2, tile3)

    m_ = [total[k:k + 1, :] for k in range(6)]
    s_ = [m_[k] + m_[k + 1] for k in range(5)]
    safe = lambda n, d, ok: jnp.where(ok, n / jnp.where(ok, d, 1.0), 0.0)
    ok0 = s_[0] > 0.0
    l10 = safe(s_[1], s_[0], ok0)
    l20 = safe(s_[2], s_[0], ok0)
    d1 = s_[2] - l10 * s_[1]
    e1 = s_[3] - l10 * s_[2]
    ok1 = d1 > 1e-6 * s_[2]
    l21 = safe(e1, d1, ok1)
    d2 = s_[4] - l20 * s_[2] - l21 * e1
    ok2 = ok1 & (d2 > 1e-6 * s_[4])
    y1 = m_[1] - l10 * m_[0]
    y2 = m_[2] - l20 * m_[0] - l21 * y1
    a2 = safe(y2, d2, ok2)
    a1 = safe(y1, d1, ok1) - l21 * a2
    a0 = safe(m_[0], s_[0], ok0) - l10 * a1 - l20 * a2
    even1 = (lanes((1, 128)) & 1) == 0
    coef = []
    for m in range(2):
        keep = even1 if m == 0 else jnp.logical_not(even1)
        coef.append([jnp.broadcast_to(jnp.where(keep, a, turn(a, 1)), (8, 128)) for a in (a0, a1, a2)])

    def last(c, carry):
        low = pl.multiple_of(c * 8, 8)
        here = pl.ds(low, 8)
        tall = pl.ds(pl.multiple_of(low + 8, 8), 8)
        for m in range(2):
            k0, k1, k2 = coef[m]
            out[0, m, here, :] = (field[SURF, m, tall, :] + k0 * basis[0, m, tall, :]
                                  + k1 * basis[1, m, tall, :] + k2 * basis[2, m, tall, :])
            out[1, m, here, :] = out[1, m, here, :] - (
                k0 * dxs[0, m, here, :] + k1 * dxs[1, m, here, :] + k2 * dxs[2, m, here, :])
            out[2, m, here, :] = out[2, m, here, :] - (
                k0 * dys[0, m, here, :] + k1 * dys[1, m, here, :] + k2 * dys[2, m, here, :])
        return carry

    lax.fori_loop(0, 8, last, 0)
    stores = [pltpu.make_async_copy(out.at[k], ref, out_sem.at[k]) for k, ref in enumerate((x_o, nu_o, nv_o))]
    for store in stores:
        store.start()
    for k, (dr, dc) in enumerate(SIDES):
        @pl.when(exists(dr, dc))
        def _():
            halo(k).wait_send()
    for s, slots in enumerate((tile1, tile2, tile3)):
        for d in range(7):
            pltpu.make_async_remote_copy(
                src_ref=slots.at[places[s]], dst_ref=slots.at[places[s]],
                send_sem=sum_send.at[s, d], recv_sem=sum_recv.at[s],
                device_id=groups[s][d], device_id_type=MESH).wait_send()
    for store in stores:
        store.wait()


def solution(mesh):
    nrow, ncol = mesh.shape["row"], mesh.shape["col"]

    def body(surface, u_face, v_face, bed_depth, wet_mask, rainfall):
        anywhere = pl.BlockSpec(memory_space=pl.ANY)
        vm = lambda *shape: pltpu.VMEM(shape, F32)
        return pl.pallas_call(
            functools.partial(kernel, nrow, ncol),
            out_shape=[jax.ShapeDtypeStruct(surface.shape, F32)] * 3,
            in_specs=[anywhere] * 6,
            out_specs=[anywhere] * 3,
            scratch_shapes=[
                vm(6, 3, TALL, 128),
                pltpu.VMEM((2, ROWS, 128), jnp.int32),
                vm(6, TALL, 128),
                vm(48, 128), vm(48, 128), vm(64, 128),
                vm(48, 128), vm(48, 128), vm(TALL, 128), vm(TALL, 128),
                vm(3, TALL, 128), vm(3, TALL, 128), vm(3, TALL, 128),
                vm(3, TALL, 128), vm(3, TALL, 128), vm(3, TALL, 128), vm(3, TALL, 128),
                vm(3, 3, TALL + 8, 128),
                vm(3, 2, ROWS, 128), vm(3, 2, ROWS, 128), vm(3, 2, ROWS, 128),
                vm(8, 8, 128), vm(8, 8, 128), vm(8, 8, 128),
                pltpu.SemaphoreType.DMA((7,)),
                pltpu.SemaphoreType.DMA((3,)),
                pltpu.SemaphoreType.DMA((8,)),
                pltpu.SemaphoreType.DMA((8,)),
                pltpu.SemaphoreType.DMA((3, 7)),
                pltpu.SemaphoreType.DMA((3,)),
            ],
            compiler_params=pltpu.CompilerParams(collective_id=0, has_side_effects=True),
        )(surface, u_face, v_face, bed_depth, wet_mask, rainfall)

    full = P(None, "row", "col")
    return jax.shard_map(body, mesh=mesh, in_specs=(full, full, full, P("row", "col"), full, full),
                         out_specs=(full, full, full), check_vma=False)
```

```python
import functools

import jax
import jax.numpy as jnp
from jax import lax
from jax.experimental import pallas as pl
from jax.experimental.pallas import tpu as pltpu
from jax.sharding import PartitionSpec as P

DTDX = 0.5
FRIC = 0.05
G1 = 4.0
CK = DTDX * G1
MESH = pl.DeviceIdType.MESH
F32 = jnp.float32

SURF, UF, VF, RAIN, WET, DEP = range(6)
SHIFT = (0, 8, 16, 48, 56, 64)
PLANES = tuple((f, m) for f in range(6) for m in range(2))
ROWS = 64
TOP = 8
TALL = 80
SIDES = ((1, 0), (-1, 0), (0, 1), (0, -1), (1, 1), (1, -1), (-1, 1), (-1, -1))


def lanes(shape):
    return lax.broadcasted_iota(jnp.int32, shape, len(shape) - 1)


def turn(x, amount):
    return pltpu.roll(x, amount % 128, x.ndim - 1)


def kernel(nrow, ncol, surf_h, u_h, v_h, bed_h, wet_h, rain_h, out,
           field, weti, own_seam, pack_n, pack_s, pack_c, got_n, got_s, got_e, got_w,
           fluxy, kx, ky, wx4, wy4, ub, vb, basis, dxs, dys,
           tile1, tile2, tile3, in_sem, send_sem, recv_sem, sum_send, sum_recv):
    r0 = lax.axis_index("row")
    c0 = lax.axis_index("col")
    y, core = r0 // 2, r0 % 2
    z, x = c0 // 4, c0 % 4
    q = x * 2 + core

    loads = [
        pltpu.make_async_copy(surf_h, field.at[SURF, 0:2, TOP:TOP + ROWS, :], in_sem.at[0]),
        pltpu.make_async_copy(u_h, field.at[UF, 0:2, TOP:TOP + ROWS, :], in_sem.at[1]),
        pltpu.make_async_copy(v_h, field.at[VF, 0:2, TOP:TOP + ROWS, :], in_sem.at[2]),
        pltpu.make_async_copy(bed_h, field.at[DEP, 0, TOP:TOP + ROWS, :], in_sem.at[3]),
        pltpu.make_async_copy(bed_h, field.at[DEP, 1, TOP:TOP + ROWS, :], in_sem.at[4]),
        pltpu.make_async_copy(wet_h, weti, in_sem.at[5]),
        pltpu.make_async_copy(rain_h, field.at[RAIN, 0:2, TOP:TOP + ROWS, :], in_sem.at[6]),
    ]
    for load in loads:
        load.start()

    def exists(dr, dc):
        ok = None
        for here, step, count in ((r0, dr, nrow), (c0, dc, ncol)):
            if step:
                there = (here + step >= 0) & (here + step < count)
                ok = there if ok is None else ok & there
        return ok

    barrier = pltpu.get_barrier_semaphore()
    groups = [
        [(r0, 4 * ((z + d) % 8) + x) for d in range(1, 8)],
        [(2 * ((y + d) % 8) + core, c0) for d in range(1, 8)],
        [(2 * y + (q + d) % 2, 4 * z + ((q + d) % 8) // 2) for d in range(1, 8)],
    ]
    places = [z, y, q]
    for dr, dc in SIDES:
        @pl.when(exists(dr, dc))
        def _():
            pl.semaphore_signal(barrier, inc=1, device_id=(r0 + dr, c0 + dc), device_id_type=MESH)
    for group in groups:
        for partner in group:
            pl.semaphore_signal(barrier, inc=1, device_id=partner, device_id_type=MESH)

    zero = lambda ref, a, b: ref.__setitem__((slice(a, b), slice(None)), jnp.zeros((b - a, 128), F32))
    for (dr, dc), ref, a, b in (
        ((1, 0), got_n, 0, 48), ((-1, 0), got_s, 0, 48),
        ((0, 1), got_e, 8, 72), ((0, -1), got_w, 8, 72),
        ((1, 1), got_e, 72, 80), ((-1, 1), got_e, 0, 8),
        ((1, -1), got_w, 72, 80), ((-1, -1), got_w, 0, 8),
    ):
        @pl.when(jnp.logical_not(exists(dr, dc)))
        def _():
            zero(ref, a, b)

    for load in loads:
        load.wait()
    for m in range(2):
        field[WET, m, TOP:TOP + ROWS, :] = weti[m].astype(F32)

    for p, (f, m) in enumerate(PLANES):
        pack_n[4 * p:4 * p + 4, :] = field[f, m, TOP + ROWS - 4:TOP + ROWS, :]
        pack_s[4 * p:4 * p + 4, :] = field[f, m, TOP:TOP + 4, :]

    def pack_columns(c, carry):
        row = pl.multiple_of(c * 8, 8)
        lane = lanes((8, 128))
        acc = jnp.zeros((8, 128), F32)
        for f, m in PLANES:
            base = SHIFT[f] + 8 + 24 * m
            rolled = turn(field[f, m, pl.ds(TOP + row, 8), :], base + 4)
            acc = jnp.where((lane >= base) & (lane < base + 8), rolled, acc)
        pack_c[pl.ds(row, 8), :] = acc
        return carry

    lax.fori_loop(0, 8, pack_columns, 0, unroll=True)

    north, south = (r0 + 1 < nrow).astype(jnp.int32), (r0 > 0).astype(jnp.int32)
    east, west = (c0 + 1 < ncol).astype(jnp.int32), (c0 > 0).astype(jnp.int32)
    peers = 21 + (1 + north + south) * (1 + east + west) - 1
    pl.semaphore_wait(barrier, peers)

    def halo(k):
        dr, dc = SIDES[k]
        if dc == 0:
            src, dst = (pack_n, got_s) if dr == 1 else (pack_s, got_n)
        else:
            lands = got_w if dc == 1 else got_e
            if dr == 0:
                src, dst = pack_c, lands.at[8:72, :]
            elif dr == 1:
                src, dst = pack_c.at[56:64, :], lands.at[0:8, :]
            else:
                src, dst = pack_c.at[0:8, :], lands.at[72:80, :]
        return pltpu.make_async_remote_copy(
            src_ref=src, dst_ref=dst, send_sem=send_sem.at[k], recv_sem=recv_sem.at[k],
            device_id=(r0 + dr, c0 + dc), device_id_type=MESH)

    for k, (dr, dc) in enumerate(SIDES):
        @pl.when(exists(dr, dc))
        def _():
            halo(k).start()

    def seam_own(row):
        lane = lanes((8, 128))
        for f in range(6):
            a = field[f, 0, pl.ds(row, 8), :]
            b = field[f, 1, pl.ds(row, 8), :]
            m0 = jnp.where(lane < 12, turn(a, 8), turn(a, 16))
            m1 = jnp.where(lane < 36, turn(b, 32), turn(b, 40))
            own_seam[f, pl.ds(row, 8), :] = jnp.where(lane < 24, m0, m1)

    def seam_body(c, carry):
        seam_own(pl.multiple_of(c * 8 + 8, 8))
        return carry

    lax.fori_loop(0, 8, seam_body, 0, unroll=True)

    def first(blocks, c, open_row=False):
        row = 5 + c * 8
        here = pl.ds(row, 8)

        def at(f, d):
            return field[f, blocks, pl.ds(row + d, 8), :]

        eta = at(SURF, 0)
        eta_n = at(SURF, 1)
        h = eta + at(DEP, 0)
        h_n = eta_n + at(DEP, 1)
        wet = at(WET, 0)
        u, u_n, u_s = at(UF, 0), at(UF, 1), at(UF, -1)
        v, v_n, v_s = at(VF, 0), at(VF, 1), at(VF, -1)
        wet_x = wet * turn(wet, -1)
        wet_y = wet * at(WET, 1)
        hx = 0.5 * (h + turn(h, -1))
        hy = 0.5 * (h + h_n)
        vs = v + v_s
        vbar = 0.25 * (vs + turn(vs, -1))
        us = u + u_n
        ubar = 0.25 * (us + turn(us, 1))
        adv_u = u * jnp.where(u > 0, u - turn(u, 1), turn(u, -1) - u)
        adv_u = adv_u + vbar * jnp.where(vbar > 0, u - u_s, u_n - u)
        adv_v = v * jnp.where(v > 0, v - v_s, v_n - v)
        adv_v = adv_v + ubar * jnp.where(ubar > 0, v - turn(v, 1), turn(v, -1) - v)
        u_star = wet_x * (u - DTDX * adv_u) / (1.0 + FRIC * jnp.abs(u))
        v_star = wet_y * (v - DTDX * adv_v) / (1.0 + FRIC * jnp.abs(v))
        kx_c = CK * hx * wet_x
        ky_c = CK * hy * wet_y
        drop_x = eta - turn(eta, -1)
        drop_y = eta - eta_n
        fx = DTDX * (hx * u_star) + kx_c * drop_x
        fy = DTDX * (hy * v_star) + ky_c * drop_y
        fluxy[blocks, here, :] = fy
        kx[blocks, here, :] = kx_c
        ky[blocks, here, :] = ky_c
        wx4[blocks, here, :] = G1 * wet_x
        wy4[blocks, here, :] = G1 * wet_y
        ub[blocks, here, :] = u_star + G1 * wet_x * drop_x
        vb[blocks, here, :] = v_star + G1 * wet_y * drop_y
        rest = at(RAIN, 0) - (fx - turn(fx, 1))
        basis[0, blocks, here, :] = rest if open_row else rest - (fy - fluxy[blocks, pl.ds(row - 1, 8), :])

    def close_row(blocks, c):
        row = 5 + c * 8
        here = pl.ds(row, 8)
        basis[0, blocks, here, :] = basis[0, blocks, here, :] - (
            fluxy[blocks, here, :] - fluxy[blocks, pl.ds(row - 1, 8), :])

    def apply(k, blocks, c):
        row = 7 + k + c * 8
        here = pl.ds(row, 8)
        below = pl.ds(row - 1, 8)
        e = basis[k, blocks, here, :]
        gx = kx[blocks, here, :] * (e - turn(e, -1))
        gy = ky[blocks, here, :] * (e - basis[k, blocks, pl.ds(row + 1, 8), :])
        gs = ky[blocks, below, :] * (basis[k, blocks, below, :] - e)
        basis[k + 1, blocks, here, :] = gx - turn(gx, 1) + (gy - gs)

    def sums(acc, blocks, c):
        row = 8 + c * 8
        here = pl.ds(row, 8)
        v0 = basis[0, blocks, here, :]
        v1 = basis[1, blocks, here, :]
        v2 = basis[2, blocks, here, :]
        dx = turn(v2, -1) - v2
        dy = basis[2, blocks, pl.ds(row + 1, 8), :] - v2
        terms = (v0 * v0, v0 * v1, v1 * v1, v1 * v2, v2 * v2,
                 kx[blocks, here, :] * (dx * dx) + ky[blocks, here, :] * (dy * dy))
        return terms if acc is None else tuple(a + t for a, t in zip(acc, terms))

    own, seam = slice(0, 2), slice(2, 3)
    for c in range(1, 8):
        first(own, c, open_row=c == 1)
    for c in range(2, 7):
        apply(0, own, c)
    for c in range(2, 6):
        apply(1, own, c)
    acc_own = None
    for c in range(2, 5):
        acc_own = sums(acc_own, own, c)

    for k, (dr, dc) in enumerate(SIDES):
        @pl.when(exists(-dr, -dc))
        def _():
            halo(k).wait_recv()

    for p, (f, m) in enumerate(PLANES):
        field[f, m, 72:76, :] = got_n[4 * p:4 * p + 4, :]
        field[f, m, 4:8, :] = got_s[4 * p:4 * p + 4, :]
    seam_own(0)
    seam_own(72)

    def seam_halo(c, carry):
        row = pl.multiple_of(c * 8, 8)
        lane = lanes((8, 128))
        both = jnp.where((lane & 4) == 0, turn(got_e[pl.ds(row, 8), :], -4), turn(got_w[pl.ds(row, 8), :], 4))
        ghost = ((lane >= 8) & (lane < 16)) | ((lane >= 32) & (lane < 40))
        for f in range(6):
            field[f, 2, pl.ds(row, 8), :] = jnp.where(ghost, turn(both, -SHIFT[f]), own_seam[f, pl.ds(row, 8), :])
        return carry

    lax.fori_loop(0, 10, seam_halo, 0, unroll=True)

    first(own, 0)
    close_row(own, 1)
    first(own, 8)
    for c in range(9):
        first(seam, c)
    for c in range(9):
        apply(0, seam, c)
    for c in (0, 1, 7, 8):
        apply(0, own, c)
    for c in range(9):
        apply(1, seam, c)
    for c in (0, 1, 6, 7, 8):
        apply(1, own, c)
    acc_seam = None
    for c in range(8):
        acc_seam = sums(acc_seam, seam, c)
    for c in (0, 1, 5, 6, 7):
        acc_own = sums(acc_own, own, c)
    lane = lanes((8, 128))
    sub = lax.broadcasted_iota(jnp.int32, (8, 128), 0)
    own_ok = (lane >= 4) & (lane < 124)
    seam_ok = [((lane >= 4 + 24 * m) & (lane < 8 + 24 * m)) | ((lane >= 16 + 24 * m) & (lane < 20 + 24 * m))
               for m in range(2)]
    rows = []
    for m in range(2):
        table = jnp.zeros((8, 128), F32)
        for k in range(6):
            part = jnp.where(own_ok, acc_own[k][m], 0.0) + jnp.where(seam_ok[m], acc_seam[k][0], 0.0)
            total = jnp.sum(part, axis=0, keepdims=True)
            table = jnp.where(sub == k, total, table)
        rows.append(table)
    even = (lane & 1) == 0
    tile = jnp.where(even, rows[0] + turn(rows[0], -1), rows[1] + turn(rows[1], 1))
    for amount in (2, 4, 8, 16, 32, 64):
        tile = tile + turn(tile, amount)

    def send_tile(s, slots, value):
        slots[places[s]] = value
        for d in range(7):
            pltpu.make_async_remote_copy(
                src_ref=slots.at[places[s]], dst_ref=slots.at[places[s]],
                send_sem=sum_send.at[s, d], recv_sem=sum_recv.at[s],
                device_id=groups[s][d], device_id_type=MESH).start()

    def take_tiles(s, slots):
        pltpu.make_async_copy(slots.at[0:7], slots.at[0:7], sum_recv.at[s]).wait()
        total = slots[0]
        for k in range(1, 8):
            total = total + slots[k]
        return total

    send_tile(0, tile1, tile)

    def join(c, carry):
        row = pl.multiple_of(8 + c * 8, 8)
        here = pl.ds(row, 8)
        lane = lanes((8, 128))

        def merged(block):
            full = []
            for m in range(2):
                west = turn(block[2], -16 - 24 * m)
                east = turn(block[2], 120 - 24 * m)
                full.append(jnp.where(lane < 4, west, jnp.where(lane >= 124, east, block[m])))
            return full

        wx_c = wx4[:, here, :]
        wy_c = wy4[:, here, :]
        for k in range(3):
            e = basis[k, :, here, :]
            e_n = basis[k, :, pl.ds(row + 1, 8), :]
            for m, value in enumerate(merged(wx_c * (turn(e, -1) - e))):
                dxs[k, m, pl.ds(row - 8, 8), :] = value
            for m, value in enumerate(merged(wy_c * (e_n - e))):
                dys[k, m, pl.ds(row - 8, 8), :] = value
            west_east = merged(e)
            for m in range(2):
                basis[k, m, here, :] = west_east[m]
        for ref, slot in ((ub, 1), (vb, 2)):
            for m, value in enumerate(merged(ref[:, here, :])):
                out[slot, m, pl.ds(row - 8, 8), :] = value
        return carry

    lax.fori_loop(0, 8, join, 0, unroll=True)

    send_tile(1, tile2, take_tiles(0, tile1))
    send_tile(2, tile3, take_tiles(1, tile2))
    total = take_tiles(2, tile3)

    m_ = [total[k:k + 1, :] for k in range(6)]
    s_ = [m_[k] + m_[k + 1] for k in range(5)]
    safe = lambda n, d, ok: jnp.where(ok, n / jnp.where(ok, d, 1.0), 0.0)
    ok0 = s_[0] > 0.0
    l10 = safe(s_[1], s_[0], ok0)
    l20 = safe(s_[2], s_[0], ok0)
    d1 = s_[2] - l10 * s_[1]
    e1 = s_[3] - l10 * s_[2]
    ok1 = d1 > 1e-6 * s_[2]
    l21 = safe(e1, d1, ok1)
    d2 = s_[4] - l20 * s_[2] - l21 * e1
    ok2 = ok1 & (d2 > 1e-6 * s_[4])
    y1 = m_[1] - l10 * m_[0]
    y2 = m_[2] - l20 * m_[0] - l21 * y1
    a2 = safe(y2, d2, ok2)
    a1 = safe(y1, d1, ok1) - l21 * a2
    a0 = safe(m_[0], s_[0], ok0) - l10 * a1 - l20 * a2
    even1 = (lanes((1, 128)) & 1) == 0
    coef = []
    for m in range(2):
        keep = even1 if m == 0 else jnp.logical_not(even1)
        coef.append([jnp.broadcast_to(jnp.where(keep, a, turn(a, 1)), (8, 128)) for a in (a0, a1, a2)])

    def last(c, carry):
        low = pl.multiple_of(c * 8, 8)
        here = pl.ds(low, 8)
        tall = pl.ds(pl.multiple_of(low + 8, 8), 8)
        for m in range(2):
            k0, k1, k2 = coef[m]
            out[0, m, here, :] = (field[SURF, m, tall, :] + k0 * basis[0, m, tall, :]
                                  + k1 * basis[1, m, tall, :] + k2 * basis[2, m, tall, :])
            out[1, m, here, :] = out[1, m, here, :] - (
                k0 * dxs[0, m, here, :] + k1 * dxs[1, m, here, :] + k2 * dxs[2, m, here, :])
            out[2, m, here, :] = out[2, m, here, :] - (
                k0 * dys[0, m, here, :] + k1 * dys[1, m, here, :] + k2 * dys[2, m, here, :])
        return carry

    lax.fori_loop(0, 8, last, 0, unroll=True)
    for k, (dr, dc) in enumerate(SIDES):
        @pl.when(exists(dr, dc))
        def _():
            halo(k).wait_send()
    for s, slots in enumerate((tile1, tile2, tile3)):
        for d in range(7):
            pltpu.make_async_remote_copy(
                src_ref=slots.at[places[s]], dst_ref=slots.at[places[s]],
                send_sem=sum_send.at[s, d], recv_sem=sum_recv.at[s],
                device_id=groups[s][d], device_id_type=MESH).wait_send()


def hand_over(fields, x_o, nu_o, nv_o, sem):
    copies = [pltpu.make_async_copy(fields.at[k], ref, sem.at[k]) for k, ref in enumerate((x_o, nu_o, nv_o))]
    for copy in copies:
        copy.start()
    for copy in copies:
        copy.wait()


def solution(mesh):
    nrow, ncol = mesh.shape["row"], mesh.shape["col"]

    def body(surface, u_face, v_face, bed_depth, wet_mask, rainfall):
        anywhere = pl.BlockSpec(memory_space=pl.ANY)
        vm = lambda *shape: pltpu.VMEM(shape, F32)
        fields = pl.pallas_call(
            functools.partial(kernel, nrow, ncol),
            out_shape=jax.ShapeDtypeStruct((3,) + surface.shape, F32),
            in_specs=[anywhere] * 6,
            out_specs=pl.BlockSpec(memory_space=pltpu.VMEM),
            scratch_shapes=[
                vm(6, 3, TALL, 128),
                pltpu.VMEM((2, ROWS, 128), jnp.int32),
                vm(6, TALL, 128),
                vm(48, 128), vm(48, 128), vm(64, 128),
                vm(48, 128), vm(48, 128), vm(TALL, 128), vm(TALL, 128),
                vm(3, TALL, 128), vm(3, TALL, 128), vm(3, TALL, 128),
                vm(3, TALL, 128), vm(3, TALL, 128), vm(3, TALL, 128), vm(3, TALL, 128),
                vm(3, 3, TALL + 8, 128),
                vm(3, 2, ROWS, 128), vm(3, 2, ROWS, 128),
                vm(8, 8, 128), vm(8, 8, 128), vm(8, 8, 128),
                pltpu.SemaphoreType.DMA((7,)),
                pltpu.SemaphoreType.DMA((8,)),
                pltpu.SemaphoreType.DMA((8,)),
                pltpu.SemaphoreType.DMA((3, 7)),
                pltpu.SemaphoreType.DMA((3,)),
            ],
            compiler_params=pltpu.CompilerParams(collective_id=0, has_side_effects=True,
                                                 vmem_limit_bytes=8 << 20),
        )(*(pltpu.with_memory_space_constraint(a, pltpu.HBM) for a in (surface, u_face, v_face, bed_depth, wet_mask, rainfall)))
        return pl.pallas_call(
            hand_over,
            out_shape=[jax.ShapeDtypeStruct(surface.shape, F32)] * 3,
            in_specs=[anywhere],
            out_specs=[anywhere] * 3,
            scratch_shapes=[pltpu.SemaphoreType.DMA((3,))],
            compiler_params=pltpu.CompilerParams(vmem_limit_bytes=1 << 20),
        )(fields)

    full = P(None, "row", "col")
    return jax.shard_map(body, mesh=mesh, in_specs=(full, full, full, P("row", "col"), full, full),
                         out_specs=(full, full, full), check_vma=False)
```

```python
import functools

import jax
import jax.numpy as jnp
from jax import lax
from jax.experimental import pallas as pl
from jax.experimental.pallas import tpu as pltpu
from jax.sharding import PartitionSpec as P

DTDX = 0.5
FRIC = 0.05
G1 = 4.0
CK = DTDX * G1
MESH = pl.DeviceIdType.MESH
F32 = jnp.float32

SURF, UF, VF, RAIN, WET, DEP = range(6)
SHIFT = (0, 8, 16, 48, 56, 64)
PLANES = tuple((f, m) for f in range(6) for m in range(2))
ROWS = 64
TOP = 8
TALL = 80
SIDES = ((1, 0), (-1, 0), (0, 1), (0, -1), (1, 1), (1, -1), (-1, 1), (-1, -1))


def lanes(shape):
    return lax.broadcasted_iota(jnp.int32, shape, len(shape) - 1)


def turn(x, amount):
    return pltpu.roll(x, amount % 128, x.ndim - 1)


def kernel(nrow, ncol, surf_h, u_h, v_h, bed_h, wet_h, rain_h, out,
           field, weti, own_seam, pack_n, pack_s, pack_c, got_n, got_s, got_e, got_w,
           fluxy, kx, ky, wx4, wy4, ub, vb, basis, dxs, dys,
           tile1, tile2, tile3, in_sem, send_sem, recv_sem, sum_send, sum_recv):
    r0 = lax.axis_index("row")
    c0 = lax.axis_index("col")
    y, core = r0 // 2, r0 % 2
    z, x = c0 // 4, c0 % 4
    q = x * 2 + core

    loads = [
        pltpu.make_async_copy(surf_h, field.at[SURF, 0:2, TOP:TOP + ROWS, :], in_sem.at[0]),
        pltpu.make_async_copy(u_h, field.at[UF, 0:2, TOP:TOP + ROWS, :], in_sem.at[1]),
        pltpu.make_async_copy(v_h, field.at[VF, 0:2, TOP:TOP + ROWS, :], in_sem.at[2]),
        pltpu.make_async_copy(bed_h, field.at[DEP, 0, TOP:TOP + ROWS, :], in_sem.at[3]),
        pltpu.make_async_copy(bed_h, field.at[DEP, 1, TOP:TOP + ROWS, :], in_sem.at[4]),
        pltpu.make_async_copy(wet_h, weti, in_sem.at[5]),
        pltpu.make_async_copy(rain_h, field.at[RAIN, 0:2, TOP:TOP + ROWS, :], in_sem.at[6]),
    ]
    for load in loads:
        load.start()

    def exists(dr, dc):
        ok = None
        for here, step, count in ((r0, dr, nrow), (c0, dc, ncol)):
            if step:
                there = (here + step >= 0) & (here + step < count)
                ok = there if ok is None else ok & there
        return ok

    barrier = pltpu.get_barrier_semaphore()
    places = [q, z, y]
    others = [[d + (d >= place).astype(jnp.int32) for d in range(7)] for place in places]
    groups = [
        [(2 * y + t % 2, 4 * z + t // 2) for t in others[0]],
        [(r0, 4 * t + x) for t in others[1]],
        [(2 * t + core, c0) for t in others[2]],
    ]
    for dr, dc in SIDES:
        @pl.when(exists(dr, dc))
        def _():
            pl.semaphore_signal(barrier, inc=1, device_id=(r0 + dr, c0 + dc), device_id_type=MESH)
    for group in groups:
        for partner in group:
            pl.semaphore_signal(barrier, inc=1, device_id=partner, device_id_type=MESH)

    zero = lambda ref, a, b: ref.__setitem__((slice(a, b), slice(None)), jnp.zeros((b - a, 128), F32))
    for (dr, dc), ref, a, b in (
        ((1, 0), got_n, 0, 48), ((-1, 0), got_s, 0, 48),
        ((0, 1), got_e, 8, 72), ((0, -1), got_w, 8, 72),
        ((1, 1), got_e, 72, 80), ((-1, 1), got_e, 0, 8),
        ((1, -1), got_w, 72, 80), ((-1, -1), got_w, 0, 8),
    ):
        @pl.when(jnp.logical_not(exists(dr, dc)))
        def _():
            zero(ref, a, b)

    for load in loads:
        load.wait()
    for m in range(2):
        field[WET, m, TOP:TOP + ROWS, :] = weti[m].astype(F32)

    for p, (f, m) in enumerate(PLANES):
        pack_n[4 * p:4 * p + 4, :] = field[f, m, TOP + ROWS - 4:TOP + ROWS, :]
        pack_s[4 * p:4 * p + 4, :] = field[f, m, TOP:TOP + 4, :]

    def pack_columns(c, carry):
        row = pl.multiple_of(c * 8, 8)
        lane = lanes((8, 128))
        acc = jnp.zeros((8, 128), F32)
        for f, m in PLANES:
            base = SHIFT[f] + 8 + 24 * m
            rolled = turn(field[f, m, pl.ds(TOP + row, 8), :], base + 4)
            acc = jnp.where((lane >= base) & (lane < base + 8), rolled, acc)
        pack_c[pl.ds(row, 8), :] = acc
        return carry

    lax.fori_loop(0, 8, pack_columns, 0, unroll=True)

    north, south = (r0 + 1 < nrow).astype(jnp.int32), (r0 > 0).astype(jnp.int32)
    east, west = (c0 + 1 < ncol).astype(jnp.int32), (c0 > 0).astype(jnp.int32)
    peers = 21 + (1 + north + south) * (1 + east + west) - 1
    pl.semaphore_wait(barrier, peers)

    def halo(k):
        dr, dc = SIDES[k]
        if dc == 0:
            src, dst = (pack_n, got_s) if dr == 1 else (pack_s, got_n)
        else:
            lands = got_w if dc == 1 else got_e
            if dr == 0:
                src, dst = pack_c, lands.at[8:72, :]
            elif dr == 1:
                src, dst = pack_c.at[56:64, :], lands.at[0:8, :]
            else:
                src, dst = pack_c.at[0:8, :], lands.at[72:80, :]
        return pltpu.make_async_remote_copy(
            src_ref=src, dst_ref=dst, send_sem=send_sem.at[k], recv_sem=recv_sem.at[k],
            device_id=(r0 + dr, c0 + dc), device_id_type=MESH)

    for k, (dr, dc) in enumerate(SIDES):
        @pl.when(exists(dr, dc))
        def _():
            halo(k).start()

    def seam_own(row):
        lane = lanes((8, 128))
        for f in range(6):
            a = field[f, 0, pl.ds(row, 8), :]
            b = field[f, 1, pl.ds(row, 8), :]
            m0 = jnp.where(lane < 12, turn(a, 8), turn(a, 16))
            m1 = jnp.where(lane < 36, turn(b, 32), turn(b, 40))
            own_seam[f, pl.ds(row, 8), :] = jnp.where(lane < 24, m0, m1)

    def seam_body(c, carry):
        seam_own(pl.multiple_of(c * 8 + 8, 8))
        return carry

    lax.fori_loop(0, 8, seam_body, 0, unroll=True)

    def first(blocks, c, open_row=False):
        row = 5 + c * 8
        here = pl.ds(row, 8)

        def at(f, d):
            return field[f, blocks, pl.ds(row + d, 8), :]

        eta = at(SURF, 0)
        eta_n = at(SURF, 1)
        h = eta + at(DEP, 0)
        h_n = eta_n + at(DEP, 1)
        wet = at(WET, 0)
        u, u_n, u_s = at(UF, 0), at(UF, 1), at(UF, -1)
        v, v_n, v_s = at(VF, 0), at(VF, 1), at(VF, -1)
        wet_x = wet * turn(wet, -1)
        wet_y = wet * at(WET, 1)
        hx = 0.5 * (h + turn(h, -1))
        hy = 0.5 * (h + h_n)
        vs = v + v_s
        vbar = 0.25 * (vs + turn(vs, -1))
        us = u + u_n
        ubar = 0.25 * (us + turn(us, 1))
        adv_u = u * jnp.where(u > 0, u - turn(u, 1), turn(u, -1) - u)
        adv_u = adv_u + vbar * jnp.where(vbar > 0, u - u_s, u_n - u)
        adv_v = v * jnp.where(v > 0, v - v_s, v_n - v)
        adv_v = adv_v + ubar * jnp.where(ubar > 0, v - turn(v, 1), turn(v, -1) - v)
        u_star = wet_x * (u - DTDX * adv_u) / (1.0 + FRIC * jnp.abs(u))
        v_star = wet_y * (v - DTDX * adv_v) / (1.0 + FRIC * jnp.abs(v))
        kx_c = CK * hx * wet_x
        ky_c = CK * hy * wet_y
        drop_x = eta - turn(eta, -1)
        drop_y = eta - eta_n
        fx = DTDX * (hx * u_star) + kx_c * drop_x
        fy = DTDX * (hy * v_star) + ky_c * drop_y
        fluxy[blocks, here, :] = fy
        kx[blocks, here, :] = kx_c
        ky[blocks, here, :] = ky_c
        wx4[blocks, here, :] = G1 * wet_x
        wy4[blocks, here, :] = G1 * wet_y
        ub[blocks, here, :] = u_star + G1 * wet_x * drop_x
        vb[blocks, here, :] = v_star + G1 * wet_y * drop_y
        rest = at(RAIN, 0) - (fx - turn(fx, 1))
        basis[0, blocks, here, :] = rest if open_row else rest - (fy - fluxy[blocks, pl.ds(row - 1, 8), :])

    def close_row(blocks, c):
        row = 5 + c * 8
        here = pl.ds(row, 8)
        basis[0, blocks, here, :] = basis[0, blocks, here, :] - (
            fluxy[blocks, here, :] - fluxy[blocks, pl.ds(row - 1, 8), :])

    def apply(k, blocks, c):
        row = 7 + k + c * 8
        here = pl.ds(row, 8)
        below = pl.ds(row - 1, 8)
        e = basis[k, blocks, here, :]
        gx = kx[blocks, here, :] * (e - turn(e, -1))
        gy = ky[blocks, here, :] * (e - basis[k, blocks, pl.ds(row + 1, 8), :])
        gs = ky[blocks, below, :] * (basis[k, blocks, below, :] - e)
        basis[k + 1, blocks, here, :] = gx - turn(gx, 1) + (gy - gs)

    def sums(acc, blocks, c):
        row = 8 + c * 8
        here = pl.ds(row, 8)
        v0 = basis[0, blocks, here, :]
        v1 = basis[1, blocks, here, :]
        v2 = basis[2, blocks, here, :]
        dx = turn(v2, -1) - v2
        dy = basis[2, blocks, pl.ds(row + 1, 8), :] - v2
        terms = (v0 * v0, v0 * v1, v1 * v1, v1 * v2, v2 * v2,
                 kx[blocks, here, :] * (dx * dx) + ky[blocks, here, :] * (dy * dy))
        return terms if acc is None else tuple(a + t for a, t in zip(acc, terms))

    own, seam = slice(0, 2), slice(2, 3)
    for c in range(1, 8):
        first(own, c, open_row=c == 1)
    for c in range(2, 7):
        apply(0, own, c)
    for c in range(2, 6):
        apply(1, own, c)
    acc_own = None
    for c in range(2, 5):
        acc_own = sums(acc_own, own, c)

    for k, (dr, dc) in enumerate(SIDES):
        @pl.when(exists(-dr, -dc))
        def _():
            halo(k).wait_recv()

    for p, (f, m) in enumerate(PLANES):
        field[f, m, 72:76, :] = got_n[4 * p:4 * p + 4, :]
        field[f, m, 4:8, :] = got_s[4 * p:4 * p + 4, :]
    seam_own(0)
    seam_own(72)

    def seam_halo(c, carry):
        row = pl.multiple_of(c * 8, 8)
        lane = lanes((8, 128))
        both = jnp.where((lane & 4) == 0, turn(got_e[pl.ds(row, 8), :], -4), turn(got_w[pl.ds(row, 8), :], 4))
        ghost = ((lane >= 8) & (lane < 16)) | ((lane >= 32) & (lane < 40))
        for f in range(6):
            field[f, 2, pl.ds(row, 8), :] = jnp.where(ghost, turn(both, -SHIFT[f]), own_seam[f, pl.ds(row, 8), :])
        return carry

    lax.fori_loop(0, 10, seam_halo, 0, unroll=True)

    first(own, 0)
    close_row(own, 1)
    first(own, 8)
    for c in range(9):
        first(seam, c)
    for c in range(9):
        apply(0, seam, c)
    for c in (0, 1, 7, 8):
        apply(0, own, c)
    for c in range(9):
        apply(1, seam, c)
    for c in (0, 1, 6, 7, 8):
        apply(1, own, c)
    acc_seam = None
    for c in range(8):
        acc_seam = sums(acc_seam, seam, c)
    for c in (0, 1, 5, 6, 7):
        acc_own = sums(acc_own, own, c)
    lane = lanes((8, 128))
    own_ok = (lane >= 4) & (lane < 124)
    seam_ok = [((lane >= 4 + 24 * m) & (lane < 8 + 24 * m)) | ((lane >= 16 + 24 * m) & (lane < 20 + 24 * m))
               for m in range(2)]
    spread = jnp.zeros((8, 128), F32)
    for m in range(2):
        for k in range(6):
            part = jnp.where(own_ok, acc_own[k][m], 0.0) + jnp.where(seam_ok[m], acc_seam[k][0], 0.0)
            spread = jnp.where(lane == 2 * k + m, jnp.sum(part, axis=1, keepdims=True), spread)
    tile = jnp.sum(spread, axis=0, keepdims=True)

    def send_tile(s, slots, value):
        slots[places[s]] = value
        for d in range(7):
            pltpu.make_async_remote_copy(
                src_ref=slots.at[places[s]], dst_ref=slots.at[places[s]],
                send_sem=sum_send.at[s, d], recv_sem=sum_recv.at[s],
                device_id=groups[s][d], device_id_type=MESH).start()

    def take_tiles(s, slots):
        pltpu.make_async_copy(slots.at[0:7], slots.at[0:7], sum_recv.at[s]).wait()
        total = slots[0]
        for k in range(1, 8):
            total = total + slots[k]
        return total

    send_tile(0, tile1, tile)

    def join(c, carry):
        row = pl.multiple_of(8 + c * 8, 8)
        here = pl.ds(row, 8)
        lane = lanes((8, 128))

        def merged(block):
            full = []
            for m in range(2):
                west = turn(block[2], -16 - 24 * m)
                east = turn(block[2], 120 - 24 * m)
                full.append(jnp.where(lane < 4, west, jnp.where(lane >= 124, east, block[m])))
            return full

        wx_c = wx4[:, here, :]
        wy_c = wy4[:, here, :]
        for k in range(3):
            e = basis[k, :, here, :]
            e_n = basis[k, :, pl.ds(row + 1, 8), :]
            for m, value in enumerate(merged(wx_c * (turn(e, -1) - e))):
                dxs[k, m, pl.ds(row - 8, 8), :] = value
            for m, value in enumerate(merged(wy_c * (e_n - e))):
                dys[k, m, pl.ds(row - 8, 8), :] = value
            west_east = merged(e)
            for m in range(2):
                basis[k, m, here, :] = west_east[m]
        for ref, slot in ((ub, 1), (vb, 2)):
            for m, value in enumerate(merged(ref[:, here, :])):
                out[slot, m, pl.ds(row - 8, 8), :] = value
        return carry

    lax.fori_loop(0, 8, join, 0, unroll=True)

    send_tile(1, tile2, take_tiles(0, tile1))
    send_tile(2, tile3, take_tiles(1, tile2))
    total = take_tiles(2, tile3)

    m_ = [turn(total, -2 * k) for k in range(6)]
    s_ = [m_[k] + m_[k + 1] for k in range(5)]
    safe = lambda n, d, ok: jnp.where(ok, n / jnp.where(ok, d, 1.0), 0.0)
    ok0 = s_[0] > 0.0
    l10 = safe(s_[1], s_[0], ok0)
    l20 = safe(s_[2], s_[0], ok0)
    d1 = s_[2] - l10 * s_[1]
    e1 = s_[3] - l10 * s_[2]
    ok1 = d1 > 1e-6 * s_[2]
    l21 = safe(e1, d1, ok1)
    d2 = s_[4] - l20 * s_[2] - l21 * e1
    ok2 = ok1 & (d2 > 1e-6 * s_[4])
    y1 = m_[1] - l10 * m_[0]
    y2 = m_[2] - l20 * m_[0] - l21 * y1
    a2 = safe(y2, d2, ok2)
    a1 = safe(y1, d1, ok1) - l21 * a2
    a0 = safe(m_[0], s_[0], ok0) - l10 * a1 - l20 * a2
    coef = [[jnp.broadcast_to(a[:, m:m + 1], (8, 128)) for a in (a0, a1, a2)] for m in range(2)]

    def last(c, carry):
        low = pl.multiple_of(c * 8, 8)
        here = pl.ds(low, 8)
        tall = pl.ds(pl.multiple_of(low + 8, 8), 8)
        for m in range(2):
            k0, k1, k2 = coef[m]
            out[0, m, here, :] = (field[SURF, m, tall, :] + k0 * basis[0, m, tall, :]
                                  + k1 * basis[1, m, tall, :] + k2 * basis[2, m, tall, :])
            out[1, m, here, :] = out[1, m, here, :] - (
                k0 * dxs[0, m, here, :] + k1 * dxs[1, m, here, :] + k2 * dxs[2, m, here, :])
            out[2, m, here, :] = out[2, m, here, :] - (
                k0 * dys[0, m, here, :] + k1 * dys[1, m, here, :] + k2 * dys[2, m, here, :])
        return carry

    lax.fori_loop(0, 8, last, 0, unroll=True)
    for k, (dr, dc) in enumerate(SIDES):
        @pl.when(exists(dr, dc))
        def _():
            halo(k).wait_send()
    for s, slots in enumerate((tile1, tile2, tile3)):
        for d in range(7):
            pltpu.make_async_remote_copy(
                src_ref=slots.at[places[s]], dst_ref=slots.at[places[s]],
                send_sem=sum_send.at[s, d], recv_sem=sum_recv.at[s],
                device_id=groups[s][d], device_id_type=MESH).wait_send()


def hand_over(fields, x_o, nu_o, nv_o, sem):
    copies = [pltpu.make_async_copy(fields.at[k], ref, sem.at[k]) for k, ref in enumerate((x_o, nu_o, nv_o))]
    for copy in copies:
        copy.start()
    for copy in copies:
        copy.wait()


def solution(mesh):
    nrow, ncol = mesh.shape["row"], mesh.shape["col"]

    def body(surface, u_face, v_face, bed_depth, wet_mask, rainfall):
        anywhere = pl.BlockSpec(memory_space=pl.ANY)
        vm = lambda *shape: pltpu.VMEM(shape, F32)
        fields = pl.pallas_call(
            functools.partial(kernel, nrow, ncol),
            out_shape=jax.ShapeDtypeStruct((3,) + surface.shape, F32),
            in_specs=[anywhere] * 6,
            out_specs=pl.BlockSpec(memory_space=pltpu.VMEM),
            scratch_shapes=[
                vm(6, 3, TALL, 128),
                pltpu.VMEM((2, ROWS, 128), jnp.int32),
                vm(6, TALL, 128),
                vm(48, 128), vm(48, 128), vm(64, 128),
                vm(48, 128), vm(48, 128), vm(TALL, 128), vm(TALL, 128),
                vm(3, TALL, 128), vm(3, TALL, 128), vm(3, TALL, 128),
                vm(3, TALL, 128), vm(3, TALL, 128), vm(3, TALL, 128), vm(3, TALL, 128),
                vm(3, 3, TALL + 8, 128),
                vm(3, 2, ROWS, 128), vm(3, 2, ROWS, 128),
                vm(8, 1, 128), vm(8, 1, 128), vm(8, 1, 128),
                pltpu.SemaphoreType.DMA((7,)),
                pltpu.SemaphoreType.DMA((8,)),
                pltpu.SemaphoreType.DMA((8,)),
                pltpu.SemaphoreType.DMA((3, 7)),
                pltpu.SemaphoreType.DMA((3,)),
            ],
            compiler_params=pltpu.CompilerParams(collective_id=0, has_side_effects=True,
                                                 vmem_limit_bytes=8 << 20),
        )(*(pltpu.with_memory_space_constraint(a, pltpu.HBM) for a in (surface, u_face, v_face, bed_depth, wet_mask, rainfall)))
        return pl.pallas_call(
            hand_over,
            out_shape=[jax.ShapeDtypeStruct(surface.shape, F32)] * 3,
            in_specs=[anywhere],
            out_specs=[anywhere] * 3,
            scratch_shapes=[pltpu.SemaphoreType.DMA((3,))],
            compiler_params=pltpu.CompilerParams(vmem_limit_bytes=1 << 20),
        )(fields)

    full = P(None, "row", "col")
    return jax.shard_map(body, mesh=mesh, in_specs=(full, full, full, P("row", "col"), full, full),
                         out_specs=(full, full, full), check_vma=False)
```

```python
import functools

import jax
import jax.numpy as jnp
from jax import lax
from jax.experimental import pallas as pl
from jax.experimental.pallas import tpu as pltpu
from jax.sharding import PartitionSpec as P

DTDX = 0.5
FRIC = 0.05
G1 = 4.0
CK = DTDX * G1
MESH = pl.DeviceIdType.MESH
F32 = jnp.float32

SURF, UF, VF, RAIN, WET, DEP = range(6)
SHIFT = (0, 8, 16, 48, 56, 64)
PLANES = tuple((f, m) for f in range(6) for m in range(2))
ROWS = 64
TOP = 8
TALL = 80
SIDES = ((1, 0), (-1, 0), (0, 1), (0, -1), (1, 1), (1, -1), (-1, 1), (-1, -1))


def lanes(shape):
    return lax.broadcasted_iota(jnp.int32, shape, len(shape) - 1)


def turn(x, amount):
    return pltpu.roll(x, amount % 128, x.ndim - 1)


def kernel(nrow, ncol, surf_h, u_h, v_h, bed_h, wet_h, rain_h, out,
           field, weti, own_seam, pack_n, pack_s, pack_c, got_n, got_s, got_e, got_w,
           fluxy, kx, ky, wx4, wy4, ub, vb, basis, dxs, dys,
           tile1, tile2, tile3, in_sem, send_sem, recv_sem, sum_send, sum_recv):
    r0 = lax.axis_index("row")
    c0 = lax.axis_index("col")
    y, core = r0 // 2, r0 % 2
    z, x = c0 // 4, c0 % 4
    q = x * 2 + core

    loads = [
        pltpu.make_async_copy(surf_h, field.at[SURF, 0:2, TOP:TOP + ROWS, :], in_sem.at[0]),
        pltpu.make_async_copy(u_h, field.at[UF, 0:2, TOP:TOP + ROWS, :], in_sem.at[1]),
        pltpu.make_async_copy(v_h, field.at[VF, 0:2, TOP:TOP + ROWS, :], in_sem.at[2]),
        pltpu.make_async_copy(bed_h, field.at[DEP, 0, TOP:TOP + ROWS, :], in_sem.at[3]),
        pltpu.make_async_copy(bed_h, field.at[DEP, 1, TOP:TOP + ROWS, :], in_sem.at[4]),
        pltpu.make_async_copy(wet_h, weti, in_sem.at[5]),
        pltpu.make_async_copy(rain_h, field.at[RAIN, 0:2, TOP:TOP + ROWS, :], in_sem.at[6]),
    ]
    for load in loads:
        load.start()

    def exists(dr, dc):
        ok = None
        for here, step, count in ((r0, dr, nrow), (c0, dc, ncol)):
            if step:
                there = (here + step >= 0) & (here + step < count)
                ok = there if ok is None else ok & there
        return ok

    barrier = pltpu.get_barrier_semaphore()
    places = [q, z, y]
    others = [[d + (d >= place).astype(jnp.int32) for d in range(7)] for place in places]
    groups = [
        [(2 * y + t % 2, 4 * z + t // 2) for t in others[0]],
        [(r0, 4 * t + x) for t in others[1]],
        [(2 * t + core, c0) for t in others[2]],
    ]
    for dr, dc in SIDES:
        @pl.when(exists(dr, dc))
        def _():
            pl.semaphore_signal(barrier, inc=1, device_id=(r0 + dr, c0 + dc), device_id_type=MESH)
    for group in groups:
        for partner in group:
            pl.semaphore_signal(barrier, inc=1, device_id=partner, device_id_type=MESH)

    zero = lambda ref, a, b: ref.__setitem__((slice(a, b), slice(None)), jnp.zeros((b - a, 128), F32))
    for (dr, dc), ref, a, b in (
        ((1, 0), got_n, 0, 48), ((-1, 0), got_s, 0, 48),
        ((0, 1), got_e, 8, 72), ((0, -1), got_w, 8, 72),
        ((1, 1), got_e, 72, 80), ((-1, 1), got_e, 0, 8),
        ((1, -1), got_w, 72, 80), ((-1, -1), got_w, 0, 8),
    ):
        @pl.when(jnp.logical_not(exists(dr, dc)))
        def _():
            zero(ref, a, b)

    for load in loads:
        load.wait()
    for m in range(2):
        field[WET, m, TOP:TOP + ROWS, :] = weti[m].astype(F32)

    for p, (f, m) in enumerate(PLANES):
        pack_n[4 * p:4 * p + 4, :] = field[f, m, TOP + ROWS - 4:TOP + ROWS, :]
        pack_s[4 * p:4 * p + 4, :] = field[f, m, TOP:TOP + 4, :]

    def pack_columns(c, carry):
        row = pl.multiple_of(c * 8, 8)
        lane = lanes((8, 128))
        acc = jnp.zeros((8, 128), F32)
        for f, m in PLANES:
            base = SHIFT[f] + 8 + 24 * m
            rolled = turn(field[f, m, pl.ds(TOP + row, 8), :], base + 4)
            acc = jnp.where((lane >= base) & (lane < base + 8), rolled, acc)
        pack_c[pl.ds(row, 8), :] = acc
        return carry

    lax.fori_loop(0, 8, pack_columns, 0, unroll=True)

    north, south = (r0 + 1 < nrow).astype(jnp.int32), (r0 > 0).astype(jnp.int32)
    east, west = (c0 + 1 < ncol).astype(jnp.int32), (c0 > 0).astype(jnp.int32)
    peers = 21 + (1 + north + south) * (1 + east + west) - 1
    pl.semaphore_wait(barrier, peers)

    def halo(k):
        dr, dc = SIDES[k]
        if dc == 0:
            src, dst = (pack_n, got_s) if dr == 1 else (pack_s, got_n)
        else:
            lands = got_w if dc == 1 else got_e
            if dr == 0:
                src, dst = pack_c, lands.at[8:72, :]
            elif dr == 1:
                src, dst = pack_c.at[56:64, :], lands.at[0:8, :]
            else:
                src, dst = pack_c.at[0:8, :], lands.at[72:80, :]
        return pltpu.make_async_remote_copy(
            src_ref=src, dst_ref=dst, send_sem=send_sem.at[k], recv_sem=recv_sem.at[k],
            device_id=(r0 + dr, c0 + dc), device_id_type=MESH)

    for k, (dr, dc) in enumerate(SIDES):
        @pl.when(exists(dr, dc))
        def _():
            halo(k).start()

    def seam_own(row):
        lane = lanes((8, 128))
        for f in range(6):
            a = field[f, 0, pl.ds(row, 8), :]
            b = field[f, 1, pl.ds(row, 8), :]
            m0 = jnp.where(lane < 12, turn(a, 8), turn(a, 16))
            m1 = jnp.where(lane < 36, turn(b, 32), turn(b, 40))
            own_seam[f, pl.ds(row, 8), :] = jnp.where(lane < 24, m0, m1)

    def seam_body(c, carry):
        seam_own(pl.multiple_of(c * 8 + 8, 8))
        return carry

    lax.fori_loop(0, 8, seam_body, 0, unroll=True)

    def first(blocks, c, open_row=False):
        row = 5 + c * 8
        here = pl.ds(row, 8)

        def at(f, d):
            return field[f, blocks, pl.ds(row + d, 8), :]

        eta = at(SURF, 0)
        eta_n = at(SURF, 1)
        h = eta + at(DEP, 0)
        h_n = eta_n + at(DEP, 1)
        wet = at(WET, 0)
        u, u_n, u_s = at(UF, 0), at(UF, 1), at(UF, -1)
        v, v_n, v_s = at(VF, 0), at(VF, 1), at(VF, -1)
        wet_x = wet * turn(wet, -1)
        wet_y = wet * at(WET, 1)
        hx = 0.5 * (h + turn(h, -1))
        hy = 0.5 * (h + h_n)
        vs = v + v_s
        vbar = 0.25 * (vs + turn(vs, -1))
        us = u + u_n
        ubar = 0.25 * (us + turn(us, 1))
        adv_u = u * jnp.where(u > 0, u - turn(u, 1), turn(u, -1) - u)
        adv_u = adv_u + vbar * jnp.where(vbar > 0, u - u_s, u_n - u)
        adv_v = v * jnp.where(v > 0, v - v_s, v_n - v)
        adv_v = adv_v + ubar * jnp.where(ubar > 0, v - turn(v, 1), turn(v, -1) - v)
        u_star = wet_x * (u - DTDX * adv_u) / (1.0 + FRIC * jnp.abs(u))
        v_star = wet_y * (v - DTDX * adv_v) / (1.0 + FRIC * jnp.abs(v))
        kx_c = CK * hx * wet_x
        ky_c = CK * hy * wet_y
        drop_x = eta - turn(eta, -1)
        drop_y = eta - eta_n
        fx = DTDX * (hx * u_star) + kx_c * drop_x
        fy = DTDX * (hy * v_star) + ky_c * drop_y
        fluxy[blocks, here, :] = fy
        kx[blocks, here, :] = kx_c
        ky[blocks, here, :] = ky_c
        wx4[blocks, here, :] = G1 * wet_x
        wy4[blocks, here, :] = G1 * wet_y
        ub[blocks, here, :] = u_star + G1 * wet_x * drop_x
        vb[blocks, here, :] = v_star + G1 * wet_y * drop_y
        rest = at(RAIN, 0) - (fx - turn(fx, 1))
        basis[0, blocks, here, :] = rest if open_row else rest - (fy - fluxy[blocks, pl.ds(row - 1, 8), :])

    def close_row(blocks, c):
        row = 5 + c * 8
        here = pl.ds(row, 8)
        basis[0, blocks, here, :] = basis[0, blocks, here, :] - (
            fluxy[blocks, here, :] - fluxy[blocks, pl.ds(row - 1, 8), :])

    def apply(k, blocks, c):
        row = 7 + k + c * 8
        here = pl.ds(row, 8)
        below = pl.ds(row - 1, 8)
        e = basis[k, blocks, here, :]
        gx = kx[blocks, here, :] * (e - turn(e, -1))
        gy = ky[blocks, here, :] * (e - basis[k, blocks, pl.ds(row + 1, 8), :])
        gs = ky[blocks, below, :] * (basis[k, blocks, below, :] - e)
        basis[k + 1, blocks, here, :] = gx - turn(gx, 1) + (gy - gs)

    def sums(acc, blocks, c):
        row = 8 + c * 8
        here = pl.ds(row, 8)
        v0 = basis[0, blocks, here, :]
        v1 = basis[1, blocks, here, :]
        v2 = basis[2, blocks, here, :]
        dx = turn(v2, -1) - v2
        dy = basis[2, blocks, pl.ds(row + 1, 8), :] - v2
        terms = (v0 * v0, v0 * v1, v1 * v1, v1 * v2, v2 * v2,
                 kx[blocks, here, :] * (dx * dx) + ky[blocks, here, :] * (dy * dy))
        return terms if acc is None else tuple(a + t for a, t in zip(acc, terms))

    own, seam = slice(0, 2), slice(2, 3)
    for c in range(1, 8):
        first(own, c, open_row=c == 1)
    for c in range(2, 7):
        apply(0, own, c)
    for c in range(2, 6):
        apply(1, own, c)
    acc_own = None
    for c in range(2, 5):
        acc_own = sums(acc_own, own, c)

    for k, (dr, dc) in enumerate(SIDES):
        @pl.when(exists(-dr, -dc))
        def _():
            halo(k).wait_recv()

    for p, (f, m) in enumerate(PLANES):
        field[f, m, 72:76, :] = got_n[4 * p:4 * p + 4, :]
        field[f, m, 4:8, :] = got_s[4 * p:4 * p + 4, :]
    seam_own(0)
    seam_own(72)

    def seam_halo(c, carry):
        row = pl.multiple_of(c * 8, 8)
        lane = lanes((8, 128))
        both = jnp.where((lane & 4) == 0, turn(got_e[pl.ds(row, 8), :], -4), turn(got_w[pl.ds(row, 8), :], 4))
        ghost = ((lane >= 8) & (lane < 16)) | ((lane >= 32) & (lane < 40))
        for f in range(6):
            field[f, 2, pl.ds(row, 8), :] = jnp.where(ghost, turn(both, -SHIFT[f]), own_seam[f, pl.ds(row, 8), :])
        return carry

    lax.fori_loop(0, 10, seam_halo, 0, unroll=True)

    first(own, 0)
    close_row(own, 1)
    first(own, 8)
    for c in range(9):
        first(seam, c)
    for c in range(9):
        apply(0, seam, c)
    for c in (0, 1, 7, 8):
        apply(0, own, c)
    for c in range(9):
        apply(1, seam, c)
    for c in (0, 1, 6, 7, 8):
        apply(1, own, c)
    acc_seam = None
    for c in range(8):
        acc_seam = sums(acc_seam, seam, c)
    for c in (0, 1, 5, 6, 7):
        acc_own = sums(acc_own, own, c)
    lane = lanes((8, 128))
    own_ok = (lane >= 4) & (lane < 124)
    seam_ok = [((lane >= 4 + 24 * m) & (lane < 8 + 24 * m)) | ((lane >= 16 + 24 * m) & (lane < 20 + 24 * m))
               for m in range(2)]
    sub = lax.broadcasted_iota(jnp.int32, (8, 128), 0)
    tables = []
    for m in range(2):
        table = jnp.zeros((8, 128), F32)
        for k in range(6):
            part = jnp.where(own_ok, acc_own[k][m], 0.0) + jnp.where(seam_ok[m], acc_seam[k][0], 0.0)
            table = jnp.where(sub == k, jnp.sum(part, axis=0, keepdims=True), table)
        tables.append(table)
    even = (lane & 1) == 0
    both_m = jnp.where(even, tables[0] + turn(tables[0], -1), tables[1] + turn(tables[1], 1))
    for amount in (2, 4, 8, 16, 32, 64):
        both_m = both_m + turn(both_m, amount)
    tile = jnp.sum(jnp.where(lane // 2 == sub, both_m, 0.0), axis=0, keepdims=True)

    def send_tile(s, slots, value):
        slots[places[s]] = value
        for d in range(7):
            pltpu.make_async_remote_copy(
                src_ref=slots.at[places[s]], dst_ref=slots.at[places[s]],
                send_sem=sum_send.at[s, d], recv_sem=sum_recv.at[s],
                device_id=groups[s][d], device_id_type=MESH).start()

    def take_tiles(s, slots):
        pltpu.make_async_copy(slots.at[0:7], slots.at[0:7], sum_recv.at[s]).wait()
        total = slots[0]
        for k in range(1, 8):
            total = total + slots[k]
        return total

    send_tile(0, tile1, tile)

    def join(c, carry):
        row = pl.multiple_of(8 + c * 8, 8)
        here = pl.ds(row, 8)
        lane = lanes((8, 128))

        def merged(block):
            full = []
            for m in range(2):
                west = turn(block[2], -16 - 24 * m)
                east = turn(block[2], 120 - 24 * m)
                full.append(jnp.where(lane < 4, west, jnp.where(lane >= 124, east, block[m])))
            return full

        wx_c = wx4[:, here, :]
        wy_c = wy4[:, here, :]
        for k in range(3):
            e = basis[k, :, here, :]
            e_n = basis[k, :, pl.ds(row + 1, 8), :]
            for m, value in enumerate(merged(wx_c * (turn(e, -1) - e))):
                dxs[k, m, pl.ds(row - 8, 8), :] = value
            for m, value in enumerate(merged(wy_c * (e_n - e))):
                dys[k, m, pl.ds(row - 8, 8), :] = value
            west_east = merged(e)
            for m in range(2):
                basis[k, m, here, :] = west_east[m]
        for ref, slot in ((ub, 1), (vb, 2)):
            for m, value in enumerate(merged(ref[:, here, :])):
                out[slot, m, pl.ds(row - 8, 8), :] = value
        return carry

    lax.fori_loop(0, 8, join, 0, unroll=2)

    send_tile(1, tile2, take_tiles(0, tile1))
    send_tile(2, tile3, take_tiles(1, tile2))
    total = take_tiles(2, tile3)

    m_ = [turn(total, -2 * k) for k in range(6)]
    s_ = [m_[k] + m_[k + 1] for k in range(5)]
    safe = lambda n, d, ok: jnp.where(ok, n / jnp.where(ok, d, 1.0), 0.0)
    ok0 = s_[0] > 0.0
    l10 = safe(s_[1], s_[0], ok0)
    l20 = safe(s_[2], s_[0], ok0)
    d1 = s_[2] - l10 * s_[1]
    e1 = s_[3] - l10 * s_[2]
    ok1 = d1 > 1e-6 * s_[2]
    l21 = safe(e1, d1, ok1)
    d2 = s_[4] - l20 * s_[2] - l21 * e1
    ok2 = ok1 & (d2 > 1e-6 * s_[4])
    y1 = m_[1] - l10 * m_[0]
    y2 = m_[2] - l20 * m_[0] - l21 * y1
    a2 = safe(y2, d2, ok2)
    a1 = safe(y1, d1, ok1) - l21 * a2
    a0 = safe(m_[0], s_[0], ok0) - l10 * a1 - l20 * a2
    coef = [[jnp.broadcast_to(a[:, m:m + 1], (8, 128)) for a in (a0, a1, a2)] for m in range(2)]

    def last(c, carry):
        low = pl.multiple_of(c * 8, 8)
        here = pl.ds(low, 8)
        tall = pl.ds(pl.multiple_of(low + 8, 8), 8)
        for m in range(2):
            k0, k1, k2 = coef[m]
            out[0, m, here, :] = (field[SURF, m, tall, :] + k0 * basis[0, m, tall, :]
                                  + k1 * basis[1, m, tall, :] + k2 * basis[2, m, tall, :])
            out[1, m, here, :] = out[1, m, here, :] - (
                k0 * dxs[0, m, here, :] + k1 * dxs[1, m, here, :] + k2 * dxs[2, m, here, :])
            out[2, m, here, :] = out[2, m, here, :] - (
                k0 * dys[0, m, here, :] + k1 * dys[1, m, here, :] + k2 * dys[2, m, here, :])
        return carry

    lax.fori_loop(0, 8, last, 0, unroll=True)
    for k, (dr, dc) in enumerate(SIDES):
        @pl.when(exists(dr, dc))
        def _():
            halo(k).wait_send()
    for s, slots in enumerate((tile1, tile2, tile3)):
        for d in range(7):
            pltpu.make_async_remote_copy(
                src_ref=slots.at[places[s]], dst_ref=slots.at[places[s]],
                send_sem=sum_send.at[s, d], recv_sem=sum_recv.at[s],
                device_id=groups[s][d], device_id_type=MESH).wait_send()


def hand_over(fields, x_o, nu_o, nv_o, sem):
    copies = [pltpu.make_async_copy(fields.at[k], ref, sem.at[k]) for k, ref in enumerate((x_o, nu_o, nv_o))]
    for copy in copies:
        copy.start()
    for copy in copies:
        copy.wait()


def solution(mesh):
    nrow, ncol = mesh.shape["row"], mesh.shape["col"]

    def body(surface, u_face, v_face, bed_depth, wet_mask, rainfall):
        anywhere = pl.BlockSpec(memory_space=pl.ANY)
        vm = lambda *shape: pltpu.VMEM(shape, F32)
        fields = pl.pallas_call(
            functools.partial(kernel, nrow, ncol),
            out_shape=jax.ShapeDtypeStruct((3,) + surface.shape, F32),
            in_specs=[anywhere] * 6,
            out_specs=pl.BlockSpec(memory_space=pltpu.VMEM),
            scratch_shapes=[
                vm(6, 3, TALL, 128),
                pltpu.VMEM((2, ROWS, 128), jnp.int32),
                vm(6, TALL, 128),
                vm(48, 128), vm(48, 128), vm(64, 128),
                vm(48, 128), vm(48, 128), vm(TALL, 128), vm(TALL, 128),
                vm(3, TALL, 128), vm(3, TALL, 128), vm(3, TALL, 128),
                vm(3, TALL, 128), vm(3, TALL, 128), vm(3, TALL, 128), vm(3, TALL, 128),
                vm(3, 3, TALL + 8, 128),
                vm(3, 2, ROWS, 128), vm(3, 2, ROWS, 128),
                vm(8, 1, 128), vm(8, 1, 128), vm(8, 1, 128),
                pltpu.SemaphoreType.DMA((7,)),
                pltpu.SemaphoreType.DMA((8,)),
                pltpu.SemaphoreType.DMA((8,)),
                pltpu.SemaphoreType.DMA((3, 7)),
                pltpu.SemaphoreType.DMA((3,)),
            ],
            compiler_params=pltpu.CompilerParams(collective_id=0, has_side_effects=True,
                                                 vmem_limit_bytes=8 << 20),
        )(*(pltpu.with_memory_space_constraint(a, pltpu.HBM) for a in (surface, u_face, v_face, bed_depth, wet_mask, rainfall)))
        return pl.pallas_call(
            hand_over,
            out_shape=[jax.ShapeDtypeStruct(surface.shape, F32)] * 3,
            in_specs=[anywhere],
            out_specs=[anywhere] * 3,
            scratch_shapes=[pltpu.SemaphoreType.DMA((3,))],
            compiler_params=pltpu.CompilerParams(vmem_limit_bytes=1 << 20),
        )(fields)

    full = P(None, "row", "col")
    return jax.shard_map(body, mesh=mesh, in_specs=(full, full, full, P("row", "col"), full, full),
                         out_specs=(full, full, full), check_vma=False)
```

```python
import functools

import jax
import jax.numpy as jnp
from jax import lax
from jax.experimental import pallas as pl
from jax.experimental.pallas import tpu as pltpu
from jax.sharding import PartitionSpec as P

DTDX = 0.5
FRIC = 0.05
G1 = 4.0
CK = DTDX * G1
MESH = pl.DeviceIdType.MESH
F32 = jnp.float32

SURF, UF, VF, RAIN, WET, DEP = range(6)
SHIFT = (0, 8, 16, 48, 56, 64)
PLANES = tuple((f, m) for f in range(6) for m in range(2))
ROWS = 64
TOP = 8
TALL = 80
SIDES = ((1, 1), (1, -1), (-1, 1), (-1, -1), (0, 1), (0, -1), (1, 0), (-1, 0))


def lanes(shape):
    return lax.broadcasted_iota(jnp.int32, shape, len(shape) - 1)


def turn(x, amount):
    return pltpu.roll(x, amount % 128, x.ndim - 1)


def kernel(nrow, ncol, surf_h, u_h, v_h, bed_h, wet_h, rain_h, out,
           field, weti, own_seam, pack_n, pack_s, pack_c, got_n, got_s, got_e, got_w,
           fluxy, kx, ky, wx4, wy4, ub, vb, basis, dxs, dys,
           tile1, tile2, tile3, in_sem, send_sem, recv_sem, sum_send, sum_recv, word):
    r0 = lax.axis_index("row")
    c0 = lax.axis_index("col")
    y, core = r0 // 2, r0 % 2
    z, x = c0 // 4, c0 % 4
    q = x * 2 + core

    loads = [
        pltpu.make_async_copy(surf_h, field.at[SURF, 0:2, TOP:TOP + ROWS, :], in_sem.at[0]),
        pltpu.make_async_copy(u_h, field.at[UF, 0:2, TOP:TOP + ROWS, :], in_sem.at[1]),
        pltpu.make_async_copy(v_h, field.at[VF, 0:2, TOP:TOP + ROWS, :], in_sem.at[2]),
        pltpu.make_async_copy(bed_h, field.at[DEP, 0, TOP:TOP + ROWS, :], in_sem.at[3]),
        pltpu.make_async_copy(bed_h, field.at[DEP, 1, TOP:TOP + ROWS, :], in_sem.at[4]),
        pltpu.make_async_copy(wet_h, weti, in_sem.at[5]),
        pltpu.make_async_copy(rain_h, field.at[RAIN, 0:2, TOP:TOP + ROWS, :], in_sem.at[6]),
    ]

    def exists(dr, dc):
        ok = None
        for here, step, count in ((r0, dr, nrow), (c0, dc, ncol)):
            if step:
                there = (here + step >= 0) & (here + step < count)
                ok = there if ok is None else ok & there
        return ok

    barrier = pltpu.get_barrier_semaphore()
    places = [q, z, y]
    others = [[d + (d >= place).astype(jnp.int32) for d in range(7)] for place in places]
    groups = [
        [(2 * y + t % 2, 4 * z + t // 2) for t in others[0]],
        [(r0, 4 * t + x) for t in others[1]],
        [(2 * t + core, c0) for t in others[2]],
    ]

    def ring(e):
        return [place for d in (e, 8 - e) for place in ((2 * ((y + d) % 8) + core, c0), (r0, 4 * ((z + d) % 8) + x))]

    for dr, dc in SIDES:
        @pl.when(exists(dr, dc))
        def _():
            pl.semaphore_signal(barrier, inc=1, device_id=(r0 + dr, c0 + dc), device_id_type=MESH)
    for partner in groups[0] + ring(1):
        pl.semaphore_signal(barrier, inc=1, device_id=partner, device_id_type=MESH)
    for load in loads:
        load.start()

    zero = lambda ref, a, b: ref.__setitem__((slice(a, b), slice(None)), jnp.zeros((b - a, 128), F32))
    for (dr, dc), ref, a, b in (
        ((1, 0), got_n, 0, 48), ((-1, 0), got_s, 0, 48),
        ((0, 1), got_e, 8, 72), ((0, -1), got_w, 8, 72),
        ((1, 1), got_e, 72, 80), ((-1, 1), got_e, 0, 8),
        ((1, -1), got_w, 72, 80), ((-1, -1), got_w, 0, 8),
    ):
        @pl.when(jnp.logical_not(exists(dr, dc)))
        def _():
            zero(ref, a, b)

    for load in loads:
        load.wait()
    for m in range(2):
        field[WET, m, TOP:TOP + ROWS, :] = weti[m].astype(F32)

    def pack_columns(c, carry):
        row = pl.multiple_of(c * 8, 8)
        lane = lanes((8, 128))
        acc = jnp.zeros((8, 128), F32)
        for f, m in PLANES:
            base = SHIFT[f] + 8 + 24 * m
            rolled = turn(field[f, m, pl.ds(TOP + row, 8), :], base + 4)
            acc = jnp.where((lane >= base) & (lane < base + 8), rolled, acc)
        pack_c[pl.ds(row, 8), :] = acc
        return carry

    lax.fori_loop(0, 8, pack_columns, 0, unroll=True)

    north, south = (r0 + 1 < nrow).astype(jnp.int32), (r0 > 0).astype(jnp.int32)
    east, west = (c0 + 1 < ncol).astype(jnp.int32), (c0 > 0).astype(jnp.int32)
    peers = 11 + (1 + north + south) * (1 + east + west) - 1
    pl.semaphore_wait(barrier, peers)

    def halo(k):
        dr, dc = SIDES[k]
        if dc == 0:
            src, dst = (pack_n, got_s) if dr == 1 else (pack_s, got_n)
        else:
            lands = got_w if dc == 1 else got_e
            if dr == 0:
                src, dst = pack_c, lands.at[8:72, :]
            elif dr == 1:
                src, dst = pack_c.at[56:64, :], lands.at[0:8, :]
            else:
                src, dst = pack_c.at[0:8, :], lands.at[72:80, :]
        return pltpu.make_async_remote_copy(
            src_ref=src, dst_ref=dst, send_sem=send_sem.at[k], recv_sem=recv_sem.at[k],
            device_id=(r0 + dr, c0 + dc), device_id_type=MESH)

    def send(some):
        for k in some:
            @pl.when(exists(*SIDES[k]))
            def _():
                halo(k).start()

    send(range(6))
    for p, (f, m) in enumerate(PLANES):
        pack_n[4 * p:4 * p + 4, :] = field[f, m, TOP + ROWS - 4:TOP + ROWS, :]
        pack_s[4 * p:4 * p + 4, :] = field[f, m, TOP:TOP + 4, :]
    send(range(6, 8))
    for partner in ring(1):
        pl.semaphore_signal(word.at[0], inc=1, device_id=partner, device_id_type=MESH)

    def seam_own(row):
        lane = lanes((8, 128))
        for f in range(6):
            a = field[f, 0, pl.ds(row, 8), :]
            b = field[f, 1, pl.ds(row, 8), :]
            m0 = jnp.where(lane < 12, turn(a, 8), turn(a, 16))
            m1 = jnp.where(lane < 36, turn(b, 32), turn(b, 40))
            own_seam[f, pl.ds(row, 8), :] = jnp.where(lane < 24, m0, m1)

    def seam_body(c, carry):
        seam_own(pl.multiple_of(c * 8 + 8, 8))
        return carry

    lax.fori_loop(0, 8, seam_body, 0, unroll=True)

    def first(blocks, c, open_row=False):
        row = 5 + c * 8
        here = pl.ds(row, 8)

        def at(f, d):
            return field[f, blocks, pl.ds(row + d, 8), :]

        eta = at(SURF, 0)
        eta_n = at(SURF, 1)
        h = eta + at(DEP, 0)
        h_n = eta_n + at(DEP, 1)
        wet = at(WET, 0)
        u, u_n, u_s = at(UF, 0), at(UF, 1), at(UF, -1)
        v, v_n, v_s = at(VF, 0), at(VF, 1), at(VF, -1)
        wet_x = wet * turn(wet, -1)
        wet_y = wet * at(WET, 1)
        hx = 0.5 * (h + turn(h, -1))
        hy = 0.5 * (h + h_n)
        vs = v + v_s
        vbar = 0.25 * (vs + turn(vs, -1))
        us = u + u_n
        ubar = 0.25 * (us + turn(us, 1))
        adv_u = u * jnp.where(u > 0, u - turn(u, 1), turn(u, -1) - u)
        adv_u = adv_u + vbar * jnp.where(vbar > 0, u - u_s, u_n - u)
        adv_v = v * jnp.where(v > 0, v - v_s, v_n - v)
        adv_v = adv_v + ubar * jnp.where(ubar > 0, v - turn(v, 1), turn(v, -1) - v)
        u_star = wet_x * (u - DTDX * adv_u) / (1.0 + FRIC * jnp.abs(u))
        v_star = wet_y * (v - DTDX * adv_v) / (1.0 + FRIC * jnp.abs(v))
        kx_c = CK * hx * wet_x
        ky_c = CK * hy * wet_y
        drop_x = eta - turn(eta, -1)
        drop_y = eta - eta_n
        fx = DTDX * (hx * u_star) + kx_c * drop_x
        fy = DTDX * (hy * v_star) + ky_c * drop_y
        fluxy[blocks, here, :] = fy
        kx[blocks, here, :] = kx_c
        ky[blocks, here, :] = ky_c
        wx4[blocks, here, :] = G1 * wet_x
        wy4[blocks, here, :] = G1 * wet_y
        ub[blocks, here, :] = u_star + G1 * wet_x * drop_x
        vb[blocks, here, :] = v_star + G1 * wet_y * drop_y
        rest = at(RAIN, 0) - (fx - turn(fx, 1))
        basis[0, blocks, here, :] = rest if open_row else rest - (fy - fluxy[blocks, pl.ds(row - 1, 8), :])

    def close_row(blocks, c):
        row = 5 + c * 8
        here = pl.ds(row, 8)
        basis[0, blocks, here, :] = basis[0, blocks, here, :] - (
            fluxy[blocks, here, :] - fluxy[blocks, pl.ds(row - 1, 8), :])

    def apply(k, blocks, c):
        row = 7 + k + c * 8
        here = pl.ds(row, 8)
        below = pl.ds(row - 1, 8)
        e = basis[k, blocks, here, :]
        gx = kx[blocks, here, :] * (e - turn(e, -1))
        gy = ky[blocks, here, :] * (e - basis[k, blocks, pl.ds(row + 1, 8), :])
        gs = ky[blocks, below, :] * (basis[k, blocks, below, :] - e)
        basis[k + 1, blocks, here, :] = gx - turn(gx, 1) + (gy - gs)

    def sums(acc, blocks, c):
        row = 8 + c * 8
        here = pl.ds(row, 8)
        v0 = basis[0, blocks, here, :]
        v1 = basis[1, blocks, here, :]
        v2 = basis[2, blocks, here, :]
        dx = turn(v2, -1) - v2
        dy = basis[2, blocks, pl.ds(row + 1, 8), :] - v2
        terms = (v0 * v0, v0 * v1, v1 * v1, v1 * v2, v2 * v2,
                 kx[blocks, here, :] * (dx * dx) + ky[blocks, here, :] * (dy * dy))
        return terms if acc is None else tuple(a + t for a, t in zip(acc, terms))

    own, seam = slice(0, 2), slice(2, 3)
    for c in range(1, 8):
        first(own, c, open_row=c == 1)
    for c in range(2, 7):
        apply(0, own, c)
    for c in range(2, 6):
        apply(1, own, c)
    acc_own = None
    for c in range(2, 5):
        acc_own = sums(acc_own, own, c)

    def receive(some):
        for k in some:
            dr, dc = SIDES[k]

            @pl.when(exists(-dr, -dc))
            def _():
                halo(k).wait_recv()

    pl.semaphore_wait(word.at[0], 4)
    for partner in ring(2):
        pl.semaphore_signal(word.at[1], inc=1, device_id=partner, device_id_type=MESH)
    receive(range(6, 8))
    for p, (f, m) in enumerate(PLANES):
        field[f, m, 72:76, :] = got_n[4 * p:4 * p + 4, :]
        field[f, m, 4:8, :] = got_s[4 * p:4 * p + 4, :]
    seam_own(0)
    seam_own(72)

    first(own, 0)
    close_row(own, 1)
    first(own, 8)
    for c in (0, 1, 7, 8):
        apply(0, own, c)
    for c in (0, 1, 6, 7, 8):
        apply(1, own, c)
    for c in (0, 1, 5, 6, 7):
        acc_own = sums(acc_own, own, c)

    receive(range(6))

    def seam_halo(c, carry):
        row = pl.multiple_of(c * 8, 8)
        lane = lanes((8, 128))
        both = jnp.where((lane & 4) == 0, turn(got_e[pl.ds(row, 8), :], -4), turn(got_w[pl.ds(row, 8), :], 4))
        ghost = ((lane >= 8) & (lane < 16)) | ((lane >= 32) & (lane < 40))
        for f in range(6):
            field[f, 2, pl.ds(row, 8), :] = jnp.where(ghost, turn(both, -SHIFT[f]), own_seam[f, pl.ds(row, 8), :])
        return carry

    lax.fori_loop(0, 10, seam_halo, 0, unroll=True)

    for c in range(9):
        first(seam, c)
    for c in range(9):
        apply(0, seam, c)
    for c in range(9):
        apply(1, seam, c)
    acc_seam = None
    for c in range(8):
        acc_seam = sums(acc_seam, seam, c)
    lane = lanes((8, 128))
    own_ok = (lane >= 4) & (lane < 124)
    seam_ok = [((lane >= 4 + 24 * m) & (lane < 8 + 24 * m)) | ((lane >= 16 + 24 * m) & (lane < 20 + 24 * m))
               for m in range(2)]
    sub = lax.broadcasted_iota(jnp.int32, (8, 128), 0)
    tables = []
    for m in range(2):
        table = jnp.zeros((8, 128), F32)
        for k in range(6):
            part = jnp.where(own_ok, acc_own[k][m], 0.0) + jnp.where(seam_ok[m], acc_seam[k][0], 0.0)
            table = jnp.where(sub == k, jnp.sum(part, axis=0, keepdims=True), table)
        tables.append(table)
    even = (lane & 1) == 0
    both_m = jnp.where(even, tables[0] + turn(tables[0], -1), tables[1] + turn(tables[1], 1))
    for step in (2, 8, 32):
        both_m = (both_m + turn(both_m, step)) + (turn(both_m, 2 * step) + turn(both_m, 3 * step))
    tile = jnp.sum(jnp.where(lane // 2 == sub, both_m, 0.0), axis=0, keepdims=True)

    def send_tile(s, slots, value):
        slots[places[s]] = value
        for d in range(7):
            pltpu.make_async_remote_copy(
                src_ref=slots.at[places[s]], dst_ref=slots.at[places[s]],
                send_sem=sum_send.at[s, d], recv_sem=sum_recv.at[s],
                device_id=groups[s][d], device_id_type=MESH).start()

    def take_tiles(s, slots):
        pltpu.make_async_copy(slots.at[0:7], slots.at[0:7], sum_recv.at[s]).wait()
        total = slots[0]
        for k in range(1, 8):
            total = total + slots[k]
        return total

    send_tile(0, tile1, tile)

    def join(c, carry):
        row = pl.multiple_of(8 + c * 8, 8)
        here = pl.ds(row, 8)
        lane = lanes((8, 128))

        def merged(block):
            full = []
            for m in range(2):
                west = turn(block[2], -16 - 24 * m)
                east = turn(block[2], 120 - 24 * m)
                full.append(jnp.where(lane < 4, west, jnp.where(lane >= 124, east, block[m])))
            return full

        wx_c = wx4[:, here, :]
        wy_c = wy4[:, here, :]
        for k in range(3):
            e = basis[k, :, here, :]
            e_n = basis[k, :, pl.ds(row + 1, 8), :]
            for m, value in enumerate(merged(wx_c * (turn(e, -1) - e))):
                dxs[k, m, pl.ds(row - 8, 8), :] = value
            for m, value in enumerate(merged(wy_c * (e_n - e))):
                dys[k, m, pl.ds(row - 8, 8), :] = value
            west_east = merged(e)
            for m in range(2):
                basis[k, m, here, :] = west_east[m]
        for ref, slot in ((ub, 1), (vb, 2)):
            for m, value in enumerate(merged(ref[:, here, :])):
                out[slot, m, pl.ds(row - 8, 8), :] = value
        return carry

    lax.fori_loop(0, 8, join, 0, unroll=2)

    pl.semaphore_wait(word.at[1], 4)
    send_tile(1, tile2, take_tiles(0, tile1))
    send_tile(2, tile3, take_tiles(1, tile2))
    total = take_tiles(2, tile3)

    m_ = [turn(total, -2 * k) for k in range(6)]
    s_ = [m_[k] + m_[k + 1] for k in range(5)]
    safe = lambda n, d, ok: jnp.where(ok, n / jnp.where(ok, d, 1.0), 0.0)
    ok0 = s_[0] > 0.0
    l10 = safe(s_[1], s_[0], ok0)
    l20 = safe(s_[2], s_[0], ok0)
    d1 = s_[2] - l10 * s_[1]
    e1 = s_[3] - l10 * s_[2]
    ok1 = d1 > 1e-6 * s_[2]
    l21 = safe(e1, d1, ok1)
    d2 = s_[4] - l20 * s_[2] - l21 * e1
    ok2 = ok1 & (d2 > 1e-6 * s_[4])
    y1 = m_[1] - l10 * m_[0]
    y2 = m_[2] - l20 * m_[0] - l21 * y1
    a2 = safe(y2, d2, ok2)
    a1 = safe(y1, d1, ok1) - l21 * a2
    a0 = safe(m_[0], s_[0], ok0) - l10 * a1 - l20 * a2
    coef = [[jnp.broadcast_to(a[:, m:m + 1], (8, 128)) for a in (a0, a1, a2)] for m in range(2)]

    def last(c, carry):
        low = pl.multiple_of(c * 8, 8)
        here = pl.ds(low, 8)
        tall = pl.ds(pl.multiple_of(low + 8, 8), 8)
        for m in range(2):
            k0, k1, k2 = coef[m]
            out[0, m, here, :] = (field[SURF, m, tall, :] + k0 * basis[0, m, tall, :]
                                  + k1 * basis[1, m, tall, :] + k2 * basis[2, m, tall, :])
            out[1, m, here, :] = out[1, m, here, :] - (
                k0 * dxs[0, m, here, :] + k1 * dxs[1, m, here, :] + k2 * dxs[2, m, here, :])
            out[2, m, here, :] = out[2, m, here, :] - (
                k0 * dys[0, m, here, :] + k1 * dys[1, m, here, :] + k2 * dys[2, m, here, :])
        return carry

    lax.fori_loop(0, 8, last, 0, unroll=True)
    for k, (dr, dc) in enumerate(SIDES):
        @pl.when(exists(dr, dc))
        def _():
            halo(k).wait_send()
    for s, slots in enumerate((tile1, tile2, tile3)):
        for d in range(7):
            pltpu.make_async_remote_copy(
                src_ref=slots.at[places[s]], dst_ref=slots.at[places[s]],
                send_sem=sum_send.at[s, d], recv_sem=sum_recv.at[s],
                device_id=groups[s][d], device_id_type=MESH).wait_send()


def hand_over(fields, x_o, nu_o, nv_o, sem):
    copies = [pltpu.make_async_copy(fields.at[k], ref, sem.at[k]) for k, ref in enumerate((x_o, nu_o, nv_o))]
    for copy in copies:
        copy.start()
    for copy in copies:
        copy.wait()


def solution(mesh):
    nrow, ncol = mesh.shape["row"], mesh.shape["col"]

    def body(surface, u_face, v_face, bed_depth, wet_mask, rainfall):
        anywhere = pl.BlockSpec(memory_space=pl.ANY)
        vm = lambda *shape: pltpu.VMEM(shape, F32)
        fields = pl.pallas_call(
            functools.partial(kernel, nrow, ncol),
            out_shape=jax.ShapeDtypeStruct((3,) + surface.shape, F32),
            in_specs=[anywhere] * 6,
            out_specs=pl.BlockSpec(memory_space=pltpu.VMEM),
            scratch_shapes=[
                vm(6, 3, TALL, 128),
                pltpu.VMEM((2, ROWS, 128), jnp.int32),
                vm(6, TALL, 128),
                vm(48, 128), vm(48, 128), vm(64, 128),
                vm(48, 128), vm(48, 128), vm(TALL, 128), vm(TALL, 128),
                vm(3, TALL, 128), vm(3, TALL, 128), vm(3, TALL, 128),
                vm(3, TALL, 128), vm(3, TALL, 128), vm(3, TALL, 128), vm(3, TALL, 128),
                vm(3, 3, TALL + 8, 128),
                vm(3, 2, ROWS, 128), vm(3, 2, ROWS, 128),
                vm(8, 1, 128), vm(8, 1, 128), vm(8, 1, 128),
                pltpu.SemaphoreType.DMA((7,)),
                pltpu.SemaphoreType.DMA((8,)),
                pltpu.SemaphoreType.DMA((8,)),
                pltpu.SemaphoreType.DMA((3, 7)),
                pltpu.SemaphoreType.DMA((3,)),
                pltpu.SemaphoreType.REGULAR((2,)),
            ],
            compiler_params=pltpu.CompilerParams(collective_id=0, has_side_effects=True,
                                                 vmem_limit_bytes=8 << 20),
        )(*(pltpu.with_memory_space_constraint(a, pltpu.HBM) for a in (surface, u_face, v_face, bed_depth, wet_mask, rainfall)))
        return pl.pallas_call(
            hand_over,
            out_shape=[jax.ShapeDtypeStruct(surface.shape, F32)] * 3,
            in_specs=[anywhere],
            out_specs=[anywhere] * 3,
            scratch_shapes=[pltpu.SemaphoreType.DMA((3,))],
            compiler_params=pltpu.CompilerParams(vmem_limit_bytes=1 << 20),
        )(fields)

    full = P(None, "row", "col")
    return jax.shard_map(body, mesh=mesh, in_specs=(full, full, full, P("row", "col"), full, full),
                         out_specs=(full, full, full), check_vma=False)
```

```python
import functools

import jax
import jax.numpy as jnp
from jax import lax
from jax.experimental import pallas as pl
from jax.experimental.pallas import tpu as pltpu
from jax.sharding import PartitionSpec as P

DTDX = 0.5
FRIC = 0.05
G1 = 4.0
CK = DTDX * G1
MESH = pl.DeviceIdType.MESH
F32 = jnp.float32

SURF, UF, VF, RAIN, WET, DEP = range(6)
SHIFT = (0, 8, 16, 48, 56, 64)
PLANES = tuple((f, m) for f in range(6) for m in range(2))
ROWS = 64
TOP = 8
TALL = 80
SIDES = ((1, 1), (1, -1), (-1, 1), (-1, -1), (0, 1), (0, -1), (1, 0), (-1, 0))


def lanes(shape):
    return lax.broadcasted_iota(jnp.int32, shape, len(shape) - 1)


def turn(x, amount):
    return pltpu.roll(x, amount % 128, x.ndim - 1)


def kernel(nrow, ncol, surf_h, u_h, v_h, bed_h, wet_h, rain_h, out,
           field, weti, own_seam, pack_n, pack_s, pack_c, got_n, got_s, got_e, got_w,
           fluxy, kx, ky, wx4, wy4, ub, vb, basis, dxs, dys,
           tile1, tile2, in_sem, send_sem, recv_sem, sum_send, sum_recv, word):
    r0 = lax.axis_index("row")
    c0 = lax.axis_index("col")
    y, core = r0 // 2, r0 % 2
    z, x = c0 // 4, c0 % 4
    q = x * 2 + core

    loads = [
        pltpu.make_async_copy(surf_h, field.at[SURF, 0:2, TOP:TOP + ROWS, :], in_sem.at[0]),
        pltpu.make_async_copy(u_h, field.at[UF, 0:2, TOP:TOP + ROWS, :], in_sem.at[1]),
        pltpu.make_async_copy(v_h, field.at[VF, 0:2, TOP:TOP + ROWS, :], in_sem.at[2]),
        pltpu.make_async_copy(bed_h, field.at[DEP, 0, TOP:TOP + ROWS, :], in_sem.at[3]),
        pltpu.make_async_copy(bed_h, field.at[DEP, 1, TOP:TOP + ROWS, :], in_sem.at[4]),
        pltpu.make_async_copy(wet_h, weti, in_sem.at[5]),
        pltpu.make_async_copy(rain_h, field.at[RAIN, 0:2, TOP:TOP + ROWS, :], in_sem.at[6]),
    ]

    def exists(dr, dc):
        ok = None
        for here, step, count in ((r0, dr, nrow), (c0, dc, ncol)):
            if step:
                there = (here + step >= 0) & (here + step < count)
                ok = there if ok is None else ok & there
        return ok

    barrier = pltpu.get_barrier_semaphore()
    near = [(q + d) % 8 for d in range(1, 8)]
    near = [(2 * y + t % 2, 4 * z + t // 2) for t in near]
    places = [r0, c0]
    others = [[d + (d >= place).astype(jnp.int32) for d in range(n - 1)] for place, n in zip(places, (nrow, ncol))]
    groups = [[(t, c0) for t in others[0]], [(r0, t) for t in others[1]]]

    def ring(e):
        return [place for d in (e, 8 - e) for place in ((2 * ((y + d) % 8) + core, c0), (r0, 4 * ((z + d) % 8) + x))]

    for dr, dc in SIDES:
        @pl.when(exists(dr, dc))
        def _():
            pl.semaphore_signal(barrier, inc=1, device_id=(r0 + dr, c0 + dc), device_id_type=MESH)
    for partner in near + ring(1):
        pl.semaphore_signal(barrier, inc=1, device_id=partner, device_id_type=MESH)
    for load in loads:
        load.start()

    zero = lambda ref, a, b: ref.__setitem__((slice(a, b), slice(None)), jnp.zeros((b - a, 128), F32))
    for (dr, dc), ref, a, b in (
        ((1, 0), got_n, 0, 48), ((-1, 0), got_s, 0, 48),
        ((0, 1), got_e, 8, 72), ((0, -1), got_w, 8, 72),
        ((1, 1), got_e, 72, 80), ((-1, 1), got_e, 0, 8),
        ((1, -1), got_w, 72, 80), ((-1, -1), got_w, 0, 8),
    ):
        @pl.when(jnp.logical_not(exists(dr, dc)))
        def _():
            zero(ref, a, b)

    for load in loads:
        load.wait()
    for m in range(2):
        field[WET, m, TOP:TOP + ROWS, :] = weti[m].astype(F32)

    def pack_columns(c, carry):
        row = pl.multiple_of(c * 8, 8)
        lane = lanes((8, 128))
        acc = jnp.zeros((8, 128), F32)
        for f, m in PLANES:
            base = SHIFT[f] + 8 + 24 * m
            rolled = turn(field[f, m, pl.ds(TOP + row, 8), :], base + 4)
            acc = jnp.where((lane >= base) & (lane < base + 8), rolled, acc)
        pack_c[pl.ds(row, 8), :] = acc
        return carry

    lax.fori_loop(0, 8, pack_columns, 0, unroll=True)

    north, south = (r0 + 1 < nrow).astype(jnp.int32), (r0 > 0).astype(jnp.int32)
    east, west = (c0 + 1 < ncol).astype(jnp.int32), (c0 > 0).astype(jnp.int32)
    peers = 11 + (1 + north + south) * (1 + east + west) - 1
    pl.semaphore_wait(barrier, peers)

    def halo(k):
        dr, dc = SIDES[k]
        if dc == 0:
            src, dst = (pack_n, got_s) if dr == 1 else (pack_s, got_n)
        else:
            lands = got_w if dc == 1 else got_e
            if dr == 0:
                src, dst = pack_c, lands.at[8:72, :]
            elif dr == 1:
                src, dst = pack_c.at[56:64, :], lands.at[0:8, :]
            else:
                src, dst = pack_c.at[0:8, :], lands.at[72:80, :]
        return pltpu.make_async_remote_copy(
            src_ref=src, dst_ref=dst, send_sem=send_sem.at[k], recv_sem=recv_sem.at[k],
            device_id=(r0 + dr, c0 + dc), device_id_type=MESH)

    def send(some):
        for k in some:
            @pl.when(exists(*SIDES[k]))
            def _():
                halo(k).start()

    send(range(6))
    for p, (f, m) in enumerate(PLANES):
        pack_n[4 * p:4 * p + 4, :] = field[f, m, TOP + ROWS - 4:TOP + ROWS, :]
        pack_s[4 * p:4 * p + 4, :] = field[f, m, TOP:TOP + 4, :]
    send(range(6, 8))
    for partner in ring(1):
        pl.semaphore_signal(word.at[0], inc=1, device_id=partner, device_id_type=MESH)

    def seam_own(row):
        lane = lanes((8, 128))
        for f in range(6):
            a = field[f, 0, pl.ds(row, 8), :]
            b = field[f, 1, pl.ds(row, 8), :]
            m0 = jnp.where(lane < 12, turn(a, 8), turn(a, 16))
            m1 = jnp.where(lane < 36, turn(b, 32), turn(b, 40))
            own_seam[f, pl.ds(row, 8), :] = jnp.where(lane < 24, m0, m1)

    def seam_body(c, carry):
        seam_own(pl.multiple_of(c * 8 + 8, 8))
        return carry

    lax.fori_loop(0, 8, seam_body, 0, unroll=True)

    def first(blocks, c, open_row=False):
        row = 5 + c * 8
        here = pl.ds(row, 8)

        def at(f, d):
            return field[f, blocks, pl.ds(row + d, 8), :]

        eta = at(SURF, 0)
        eta_n = at(SURF, 1)
        h = eta + at(DEP, 0)
        h_n = eta_n + at(DEP, 1)
        wet = at(WET, 0)
        u, u_n, u_s = at(UF, 0), at(UF, 1), at(UF, -1)
        v, v_n, v_s = at(VF, 0), at(VF, 1), at(VF, -1)
        wet_x = wet * turn(wet, -1)
        wet_y = wet * at(WET, 1)
        hx = 0.5 * (h + turn(h, -1))
        hy = 0.5 * (h + h_n)
        vs = v + v_s
        vbar = 0.25 * (vs + turn(vs, -1))
        us = u + u_n
        ubar = 0.25 * (us + turn(us, 1))
        adv_u = u * jnp.where(u > 0, u - turn(u, 1), turn(u, -1) - u)
        adv_u = adv_u + vbar * jnp.where(vbar > 0, u - u_s, u_n - u)
        adv_v = v * jnp.where(v > 0, v - v_s, v_n - v)
        adv_v = adv_v + ubar * jnp.where(ubar > 0, v - turn(v, 1), turn(v, -1) - v)
        u_star = wet_x * (u - DTDX * adv_u) / (1.0 + FRIC * jnp.abs(u))
        v_star = wet_y * (v - DTDX * adv_v) / (1.0 + FRIC * jnp.abs(v))
        kx_c = CK * hx * wet_x
        ky_c = CK * hy * wet_y
        drop_x = eta - turn(eta, -1)
        drop_y = eta - eta_n
        fx = DTDX * (hx * u_star) + kx_c * drop_x
        fy = DTDX * (hy * v_star) + ky_c * drop_y
        fluxy[blocks, here, :] = fy
        kx[blocks, here, :] = kx_c
        ky[blocks, here, :] = ky_c
        wx4[blocks, here, :] = G1 * wet_x
        wy4[blocks, here, :] = G1 * wet_y
        ub[blocks, here, :] = u_star + G1 * wet_x * drop_x
        vb[blocks, here, :] = v_star + G1 * wet_y * drop_y
        rest = at(RAIN, 0) - (fx - turn(fx, 1))
        basis[0, blocks, here, :] = rest if open_row else rest - (fy - fluxy[blocks, pl.ds(row - 1, 8), :])

    def close_row(blocks, c):
        row = 5 + c * 8
        here = pl.ds(row, 8)
        basis[0, blocks, here, :] = basis[0, blocks, here, :] - (
            fluxy[blocks, here, :] - fluxy[blocks, pl.ds(row - 1, 8), :])

    def apply(k, blocks, c):
        row = 7 + k + c * 8
        here = pl.ds(row, 8)
        below = pl.ds(row - 1, 8)
        e = basis[k, blocks, here, :]
        gx = kx[blocks, here, :] * (e - turn(e, -1))
        gy = ky[blocks, here, :] * (e - basis[k, blocks, pl.ds(row + 1, 8), :])
        gs = ky[blocks, below, :] * (basis[k, blocks, below, :] - e)
        basis[k + 1, blocks, here, :] = gx - turn(gx, 1) + (gy - gs)

    def sums(acc, blocks, c):
        row = 8 + c * 8
        here = pl.ds(row, 8)
        v0 = basis[0, blocks, here, :]
        v1 = basis[1, blocks, here, :]
        v2 = basis[2, blocks, here, :]
        dx = turn(v2, -1) - v2
        dy = basis[2, blocks, pl.ds(row + 1, 8), :] - v2
        terms = (v0 * v0, v0 * v1, v1 * v1, v1 * v2, v2 * v2,
                 kx[blocks, here, :] * (dx * dx) + ky[blocks, here, :] * (dy * dy))
        return terms if acc is None else tuple(a + t for a, t in zip(acc, terms))

    own, seam = slice(0, 2), slice(2, 3)
    for c in range(1, 8):
        first(own, c, open_row=c == 1)
    for c in range(2, 7):
        apply(0, own, c)
    for c in range(2, 6):
        apply(1, own, c)
    acc_own = None
    for c in range(2, 5):
        acc_own = sums(acc_own, own, c)

    def receive(some):
        for k in some:
            dr, dc = SIDES[k]

            @pl.when(exists(-dr, -dc))
            def _():
                halo(k).wait_recv()

    pl.semaphore_wait(word.at[0], 4)
    for partner in ring(2):
        pl.semaphore_signal(word.at[1], inc=1, device_id=partner, device_id_type=MESH)
    receive(range(6, 8))
    for p, (f, m) in enumerate(PLANES):
        field[f, m, 72:76, :] = got_n[4 * p:4 * p + 4, :]
        field[f, m, 4:8, :] = got_s[4 * p:4 * p + 4, :]
    seam_own(0)
    seam_own(72)

    first(own, 0)
    close_row(own, 1)
    first(own, 8)
    for c in (0, 1, 7, 8):
        apply(0, own, c)
    for c in (0, 1, 6, 7, 8):
        apply(1, own, c)
    for c in (0, 1, 5, 6, 7):
        acc_own = sums(acc_own, own, c)

    pl.semaphore_wait(word.at[1], 4)
    for partner in ring(1):
        pl.semaphore_signal(word.at[2], inc=1, device_id=partner, device_id_type=MESH)
    receive(range(6))

    def seam_halo(c, carry):
        row = pl.multiple_of(c * 8, 8)
        lane = lanes((8, 128))
        both = jnp.where((lane & 4) == 0, turn(got_e[pl.ds(row, 8), :], -4), turn(got_w[pl.ds(row, 8), :], 4))
        ghost = ((lane >= 8) & (lane < 16)) | ((lane >= 32) & (lane < 40))
        for f in range(6):
            field[f, 2, pl.ds(row, 8), :] = jnp.where(ghost, turn(both, -SHIFT[f]), own_seam[f, pl.ds(row, 8), :])
        return carry

    lax.fori_loop(0, 10, seam_halo, 0, unroll=True)

    for c in range(9):
        first(seam, c)
    for c in range(9):
        apply(0, seam, c)
    for c in range(9):
        apply(1, seam, c)
    acc_seam = None
    for c in range(8):
        acc_seam = sums(acc_seam, seam, c)
    lane = lanes((8, 128))
    own_ok = (lane >= 4) & (lane < 124)
    seam_ok = [((lane >= 4 + 24 * m) & (lane < 8 + 24 * m)) | ((lane >= 16 + 24 * m) & (lane < 20 + 24 * m))
               for m in range(2)]
    sub = lax.broadcasted_iota(jnp.int32, (8, 128), 0)
    tables = []
    for m in range(2):
        table = jnp.zeros((8, 128), F32)
        for k in range(6):
            part = jnp.where(own_ok, acc_own[k][m], 0.0) + jnp.where(seam_ok[m], acc_seam[k][0], 0.0)
            table = jnp.where(sub == k, jnp.sum(part, axis=0, keepdims=True), table)
        tables.append(table)
    even = (lane & 1) == 0
    both_m = jnp.where(even, tables[0] + turn(tables[0], -1), tables[1] + turn(tables[1], 1))
    for step in (2, 8, 32):
        both_m = (both_m + turn(both_m, step)) + (turn(both_m, 2 * step) + turn(both_m, 3 * step))
    tile = jnp.sum(jnp.where(lane // 2 == sub, both_m, 0.0), axis=0, keepdims=True)

    def send_tile(s, slots, value):
        slots[places[s]] = value
        for partner in groups[s]:
            pltpu.make_async_remote_copy(
                src_ref=slots.at[places[s]], dst_ref=slots.at[places[s]],
                send_sem=sum_send.at[s], recv_sem=sum_recv.at[s],
                device_id=partner, device_id_type=MESH).start()

    def wait_all(slots, sem):
        rest = slots.at[0:slots.shape[0] - 1]
        pltpu.make_async_copy(rest, rest, sem).wait()

    def take_tiles(s, slots):
        wait_all(slots, sum_recv.at[s])
        terms = [slots[k] for k in range(slots.shape[0])]
        while len(terms) > 1:
            terms = [a + b for a, b in zip(terms[::2], terms[1::2])]
        return terms[0]

    pl.semaphore_wait(word.at[2], 4)
    send_tile(0, tile1, tile)

    def join(c, carry):
        row = pl.multiple_of(8 + c * 8, 8)
        here = pl.ds(row, 8)
        lane = lanes((8, 128))

        def merged(block):
            full = []
            for m in range(2):
                west = turn(block[2], -16 - 24 * m)
                east = turn(block[2], 120 - 24 * m)
                full.append(jnp.where(lane < 4, west, jnp.where(lane >= 124, east, block[m])))
            return full

        wx_c = wx4[:, here, :]
        wy_c = wy4[:, here, :]
        for k in range(3):
            e = basis[k, :, here, :]
            e_n = basis[k, :, pl.ds(row + 1, 8), :]
            for m, value in enumerate(merged(wx_c * (turn(e, -1) - e))):
                dxs[k, m, pl.ds(row - 8, 8), :] = value
            for m, value in enumerate(merged(wy_c * (e_n - e))):
                dys[k, m, pl.ds(row - 8, 8), :] = value
            west_east = merged(e)
            for m in range(2):
                basis[k, m, here, :] = west_east[m]
        for ref, slot in ((ub, 1), (vb, 2)):
            for m, value in enumerate(merged(ref[:, here, :])):
                out[slot, m, pl.ds(row - 8, 8), :] = value
        return carry

    lax.fori_loop(0, 8, join, 0, unroll=2)

    send_tile(1, tile2, take_tiles(0, tile1))
    total = take_tiles(1, tile2)

    m_ = [turn(total, -2 * k) for k in range(6)]
    s_ = [m_[k] + m_[k + 1] for k in range(5)]
    safe = lambda n, d, ok: jnp.where(ok, n / jnp.where(ok, d, 1.0), 0.0)
    ok0 = s_[0] > 0.0
    l10 = safe(s_[1], s_[0], ok0)
    l20 = safe(s_[2], s_[0], ok0)
    d1 = s_[2] - l10 * s_[1]
    e1 = s_[3] - l10 * s_[2]
    ok1 = d1 > 1e-6 * s_[2]
    l21 = safe(e1, d1, ok1)
    d2 = s_[4] - l20 * s_[2] - l21 * e1
    ok2 = ok1 & (d2 > 1e-6 * s_[4])
    y1 = m_[1] - l10 * m_[0]
    y2 = m_[2] - l20 * m_[0] - l21 * y1
    a2 = safe(y2, d2, ok2)
    a1 = safe(y1, d1, ok1) - l21 * a2
    a0 = safe(m_[0], s_[0], ok0) - l10 * a1 - l20 * a2
    coef = [[jnp.broadcast_to(a[:, m:m + 1], (8, 128)) for a in (a0, a1, a2)] for m in range(2)]

    def last(c, carry):
        low = pl.multiple_of(c * 8, 8)
        here = pl.ds(low, 8)
        tall = pl.ds(pl.multiple_of(low + 8, 8), 8)
        for m in range(2):
            k0, k1, k2 = coef[m]
            out[0, m, here, :] = (field[SURF, m, tall, :] + k0 * basis[0, m, tall, :]
                                  + k1 * basis[1, m, tall, :] + k2 * basis[2, m, tall, :])
            out[1, m, here, :] = out[1, m, here, :] - (
                k0 * dxs[0, m, here, :] + k1 * dxs[1, m, here, :] + k2 * dxs[2, m, here, :])
            out[2, m, here, :] = out[2, m, here, :] - (
                k0 * dys[0, m, here, :] + k1 * dys[1, m, here, :] + k2 * dys[2, m, here, :])
        return carry

    lax.fori_loop(0, 8, last, 0, unroll=True)
    for k, (dr, dc) in enumerate(SIDES):
        @pl.when(exists(dr, dc))
        def _():
            halo(k).wait_send()
    for s, slots in enumerate((tile1, tile2)):
        wait_all(slots, sum_send.at[s])


def hand_over(fields, x_o, nu_o, nv_o, sem):
    copies = [pltpu.make_async_copy(fields.at[k], ref, sem.at[k]) for k, ref in enumerate((x_o, nu_o, nv_o))]
    for copy in copies:
        copy.start()
    for copy in copies:
        copy.wait()


def solution(mesh):
    nrow, ncol = mesh.shape["row"], mesh.shape["col"]

    def body(surface, u_face, v_face, bed_depth, wet_mask, rainfall):
        anywhere = pl.BlockSpec(memory_space=pl.ANY)
        vm = lambda *shape: pltpu.VMEM(shape, F32)
        fields = pl.pallas_call(
            functools.partial(kernel, nrow, ncol),
            out_shape=jax.ShapeDtypeStruct((3,) + surface.shape, F32),
            in_specs=[anywhere] * 6,
            out_specs=pl.BlockSpec(memory_space=pltpu.VMEM),
            scratch_shapes=[
                vm(6, 3, TALL, 128),
                pltpu.VMEM((2, ROWS, 128), jnp.int32),
                vm(6, TALL, 128),
                vm(48, 128), vm(48, 128), vm(64, 128),
                vm(48, 128), vm(48, 128), vm(TALL, 128), vm(TALL, 128),
                vm(3, TALL, 128), vm(3, TALL, 128), vm(3, TALL, 128),
                vm(3, TALL, 128), vm(3, TALL, 128), vm(3, TALL, 128), vm(3, TALL, 128),
                vm(3, 3, TALL + 8, 128),
                vm(3, 2, ROWS, 128), vm(3, 2, ROWS, 128),
                vm(nrow, 1, 128), vm(ncol, 1, 128),
                pltpu.SemaphoreType.DMA((7,)),
                pltpu.SemaphoreType.DMA((8,)),
                pltpu.SemaphoreType.DMA((8,)),
                pltpu.SemaphoreType.DMA((2,)),
                pltpu.SemaphoreType.DMA((2,)),
                pltpu.SemaphoreType.REGULAR((3,)),
            ],
            compiler_params=pltpu.CompilerParams(collective_id=0, has_side_effects=True,
                                                 vmem_limit_bytes=8 << 20),
        )(*(pltpu.with_memory_space_constraint(a, pltpu.HBM) for a in (surface, u_face, v_face, bed_depth, wet_mask, rainfall)))
        return pl.pallas_call(
            hand_over,
            out_shape=[jax.ShapeDtypeStruct(surface.shape, F32)] * 3,
            in_specs=[anywhere],
            out_specs=[anywhere] * 3,
            scratch_shapes=[pltpu.SemaphoreType.DMA((3,))],
            compiler_params=pltpu.CompilerParams(vmem_limit_bytes=1 << 20),
        )(fields)

    full = P(None, "row", "col")
    return jax.shard_map(body, mesh=mesh, in_specs=(full, full, full, P("row", "col"), full, full),
                         out_specs=(full, full, full), check_vma=False)
```

```python
import functools

import jax
import jax.numpy as jnp
from jax import lax
from jax.experimental import pallas as pl
from jax.experimental.pallas import tpu as pltpu
from jax.sharding import PartitionSpec as P

DTDX = 0.5
FRIC = 0.05
G1 = 4.0
CK = DTDX * G1
MESH = pl.DeviceIdType.MESH
F32 = jnp.float32

SURF, UF, VF, RAIN, WET, DEP = range(6)
SHIFT = (0, 8, 16, 48, 56, 64)
PLANES = tuple((f, m) for f in range(6) for m in range(2))
ROWS = 64
TOP = 8
TALL = 80
SIDES = ((1, 1), (1, -1), (-1, 1), (-1, -1), (0, 1), (0, -1), (1, 0), (-1, 0))


def lanes(shape):
    return lax.broadcasted_iota(jnp.int32, shape, len(shape) - 1)


def turn(x, amount):
    return pltpu.roll(x, amount % 128, x.ndim - 1)


def kernel(nrow, ncol, surf_h, u_h, v_h, bed_h, wet_h, rain_h, out,
           field, weti, own_seam, pack_n, pack_s, pack_c, got_n, got_s, got_e, got_w,
           fluxy, kx, ky, wx4, wy4, ub, vb, basis, dxs, dys,
           tile1, tile2, in_sem, send_sem, recv_sem, sum_send, sum_recv, word):
    r0 = lax.axis_index("row")
    c0 = lax.axis_index("col")
    y, core = r0 // 2, r0 % 2
    z, x = c0 // 4, c0 % 4
    q = x * 2 + core

    loads = [
        pltpu.make_async_copy(surf_h, field.at[SURF, 0:2, TOP:TOP + ROWS, :], in_sem.at[0]),
        pltpu.make_async_copy(u_h, field.at[UF, 0:2, TOP:TOP + ROWS, :], in_sem.at[1]),
        pltpu.make_async_copy(v_h, field.at[VF, 0:2, TOP:TOP + ROWS, :], in_sem.at[2]),
        pltpu.make_async_copy(bed_h, field.at[DEP, 0, TOP:TOP + ROWS, :], in_sem.at[3]),
        pltpu.make_async_copy(bed_h, field.at[DEP, 1, TOP:TOP + ROWS, :], in_sem.at[4]),
        pltpu.make_async_copy(wet_h, weti, in_sem.at[5]),
        pltpu.make_async_copy(rain_h, field.at[RAIN, 0:2, TOP:TOP + ROWS, :], in_sem.at[6]),
    ]

    def exists(dr, dc):
        ok = None
        for here, step, count in ((r0, dr, nrow), (c0, dc, ncol)):
            if step:
                there = (here + step >= 0) & (here + step < count)
                ok = there if ok is None else ok & there
        return ok

    barrier = pltpu.get_barrier_semaphore()
    near = [(q + d) % 8 for d in range(1, 8)]
    near = [(2 * y + t % 2, 4 * z + t // 2) for t in near]
    places = [r0, c0]
    others = [[d + (d >= place).astype(jnp.int32) for d in range(n - 1)] for place, n in zip(places, (nrow, ncol))]
    groups = [[(t, c0) for t in others[0]], [(r0, t) for t in others[1]]]

    def ring(e):
        return [place for d in (e, 8 - e) for place in ((2 * ((y + d) % 8) + core, c0), (r0, 4 * ((z + d) % 8) + x))]

    for dr, dc in SIDES:
        @pl.when(exists(dr, dc))
        def _():
            pl.semaphore_signal(barrier, inc=1, device_id=(r0 + dr, c0 + dc), device_id_type=MESH)
    for partner in ring(1):
        pl.semaphore_signal(barrier, inc=1, device_id=partner, device_id_type=MESH)
    for load in loads:
        load.start()
    for partner in near:
        pl.semaphore_signal(barrier, inc=1, device_id=partner, device_id_type=MESH)

    zero = lambda ref, a, b: ref.__setitem__((slice(a, b), slice(None)), jnp.zeros((b - a, 128), F32))
    for (dr, dc), ref, a, b in (
        ((1, 0), got_n, 0, 48), ((-1, 0), got_s, 0, 48),
        ((0, 1), got_e, 8, 72), ((0, -1), got_w, 8, 72),
        ((1, 1), got_e, 72, 80), ((-1, 1), got_e, 0, 8),
        ((1, -1), got_w, 72, 80), ((-1, -1), got_w, 0, 8),
    ):
        @pl.when(jnp.logical_not(exists(dr, dc)))
        def _():
            zero(ref, a, b)

    for load in loads:
        load.wait()
    for m in range(2):
        field[WET, m, TOP:TOP + ROWS, :] = weti[m].astype(F32)

    def pack_columns(c, carry):
        row = pl.multiple_of(c * 8, 8)
        lane = lanes((8, 128))
        acc = jnp.zeros((8, 128), F32)
        for f, m in PLANES:
            base = SHIFT[f] + 8 + 24 * m
            rolled = turn(field[f, m, pl.ds(TOP + row, 8), :], base + 4)
            acc = jnp.where((lane >= base) & (lane < base + 8), rolled, acc)
        pack_c[pl.ds(row, 8), :] = acc
        return carry

    lax.fori_loop(0, 8, pack_columns, 0, unroll=True)

    north, south = (r0 + 1 < nrow).astype(jnp.int32), (r0 > 0).astype(jnp.int32)
    east, west = (c0 + 1 < ncol).astype(jnp.int32), (c0 > 0).astype(jnp.int32)
    peers = 11 + (1 + north + south) * (1 + east + west) - 1
    pl.semaphore_wait(barrier, peers)

    def halo(k):
        dr, dc = SIDES[k]
        if dc == 0:
            src, dst = (pack_n, got_s) if dr == 1 else (pack_s, got_n)
        else:
            lands = got_w if dc == 1 else got_e
            if dr == 0:
                src, dst = pack_c, lands.at[8:72, :]
            elif dr == 1:
                src, dst = pack_c.at[56:64, :], lands.at[0:8, :]
            else:
                src, dst = pack_c.at[0:8, :], lands.at[72:80, :]
        return pltpu.make_async_remote_copy(
            src_ref=src, dst_ref=dst, send_sem=send_sem.at[k], recv_sem=recv_sem.at[k],
            device_id=(r0 + dr, c0 + dc), device_id_type=MESH)

    def send(some):
        for k in some:
            @pl.when(exists(*SIDES[k]))
            def _():
                halo(k).start()

    send(range(6))
    for p, (f, m) in enumerate(PLANES):
        pack_n[4 * p:4 * p + 4, :] = field[f, m, TOP + ROWS - 4:TOP + ROWS, :]
        pack_s[4 * p:4 * p + 4, :] = field[f, m, TOP:TOP + 4, :]
    send(range(6, 8))
    for partner in ring(1):
        pl.semaphore_signal(word.at[0], inc=1, device_id=partner, device_id_type=MESH)

    def seam_own(row):
        lane = lanes((8, 128))
        for f in range(6):
            a = field[f, 0, pl.ds(row, 8), :]
            b = field[f, 1, pl.ds(row, 8), :]
            m0 = jnp.where(lane < 12, turn(a, 8), turn(a, 16))
            m1 = jnp.where(lane < 36, turn(b, 32), turn(b, 40))
            own_seam[f, pl.ds(row, 8), :] = jnp.where(lane < 24, m0, m1)

    def seam_body(c, carry):
        seam_own(pl.multiple_of(c * 8 + 8, 8))
        return carry

    lax.fori_loop(0, 8, seam_body, 0, unroll=True)

    def first(blocks, c, open_row=False):
        row = 5 + c * 8
        here = pl.ds(row, 8)

        def at(f, d):
            return field[f, blocks, pl.ds(row + d, 8), :]

        eta = at(SURF, 0)
        eta_n = at(SURF, 1)
        h = eta + at(DEP, 0)
        h_n = eta_n + at(DEP, 1)
        wet = at(WET, 0)
        u, u_n, u_s = at(UF, 0), at(UF, 1), at(UF, -1)
        v, v_n, v_s = at(VF, 0), at(VF, 1), at(VF, -1)
        wet_x = wet * turn(wet, -1)
        wet_y = wet * at(WET, 1)
        hx = 0.5 * (h + turn(h, -1))
        hy = 0.5 * (h + h_n)
        vs = v + v_s
        vbar = 0.25 * (vs + turn(vs, -1))
        us = u + u_n
        ubar = 0.25 * (us + turn(us, 1))
        adv_u = u * jnp.where(u > 0, u - turn(u, 1), turn(u, -1) - u)
        adv_u = adv_u + vbar * jnp.where(vbar > 0, u - u_s, u_n - u)
        adv_v = v * jnp.where(v > 0, v - v_s, v_n - v)
        adv_v = adv_v + ubar * jnp.where(ubar > 0, v - turn(v, 1), turn(v, -1) - v)
        u_star = wet_x * (u - DTDX * adv_u) / (1.0 + FRIC * jnp.abs(u))
        v_star = wet_y * (v - DTDX * adv_v) / (1.0 + FRIC * jnp.abs(v))
        kx_c = CK * hx * wet_x
        ky_c = CK * hy * wet_y
        drop_x = eta - turn(eta, -1)
        drop_y = eta - eta_n
        fx = DTDX * (hx * u_star) + kx_c * drop_x
        fy = DTDX * (hy * v_star) + ky_c * drop_y
        fluxy[blocks, here, :] = fy
        kx[blocks, here, :] = kx_c
        ky[blocks, here, :] = ky_c
        wx4[blocks, here, :] = G1 * wet_x
        wy4[blocks, here, :] = G1 * wet_y
        ub[blocks, here, :] = u_star + G1 * wet_x * drop_x
        vb[blocks, here, :] = v_star + G1 * wet_y * drop_y
        rest = at(RAIN, 0) - (fx - turn(fx, 1))
        basis[0, blocks, here, :] = rest if open_row else rest - (fy - fluxy[blocks, pl.ds(row - 1, 8), :])

    def close_row(blocks, c):
        row = 5 + c * 8
        here = pl.ds(row, 8)
        basis[0, blocks, here, :] = basis[0, blocks, here, :] - (
            fluxy[blocks, here, :] - fluxy[blocks, pl.ds(row - 1, 8), :])

    def apply(k, blocks, c):
        row = 7 + k + c * 8
        here = pl.ds(row, 8)
        below = pl.ds(row - 1, 8)
        e = basis[k, blocks, here, :]
        gx = kx[blocks, here, :] * (e - turn(e, -1))
        gy = ky[blocks, here, :] * (e - basis[k, blocks, pl.ds(row + 1, 8), :])
        gs = ky[blocks, below, :] * (basis[k, blocks, below, :] - e)
        basis[k + 1, blocks, here, :] = gx - turn(gx, 1) + (gy - gs)

    def sums(acc, blocks, c):
        row = 8 + c * 8
        here = pl.ds(row, 8)
        v0 = basis[0, blocks, here, :]
        v1 = basis[1, blocks, here, :]
        v2 = basis[2, blocks, here, :]
        dx = turn(v2, -1) - v2
        dy = basis[2, blocks, pl.ds(row + 1, 8), :] - v2
        terms = (v0 * v0, v0 * v1, v1 * v1, v1 * v2, v2 * v2,
                 kx[blocks, here, :] * (dx * dx) + ky[blocks, here, :] * (dy * dy))
        return terms if acc is None else tuple(a + t for a, t in zip(acc, terms))

    own, seam = slice(0, 2), slice(2, 3)
    for c in range(1, 8):
        first(own, c, open_row=c == 1)
    for c in range(2, 7):
        apply(0, own, c)
    for c in range(2, 6):
        apply(1, own, c)
    acc_own = None
    for c in range(2, 5):
        acc_own = sums(acc_own, own, c)

    def receive(some):
        for k in some:
            dr, dc = SIDES[k]

            @pl.when(exists(-dr, -dc))
            def _():
                halo(k).wait_recv()

    pl.semaphore_wait(word.at[0], 4)
    for partner in ring(2):
        pl.semaphore_signal(word.at[1], inc=1, device_id=partner, device_id_type=MESH)
    receive(range(6, 8))
    for p, (f, m) in enumerate(PLANES):
        field[f, m, 72:76, :] = got_n[4 * p:4 * p + 4, :]
        field[f, m, 4:8, :] = got_s[4 * p:4 * p + 4, :]
    seam_own(0)
    seam_own(72)

    first(own, 0)
    close_row(own, 1)
    first(own, 8)
    for c in (0, 1, 7, 8):
        apply(0, own, c)
    for c in (0, 1, 6, 7, 8):
        apply(1, own, c)
    for c in (0, 1, 5, 6, 7):
        acc_own = sums(acc_own, own, c)

    pl.semaphore_wait(word.at[1], 4)
    for partner in ring(1):
        pl.semaphore_signal(word.at[2], inc=1, device_id=partner, device_id_type=MESH)
    receive(range(6))

    def seam_halo(c, carry):
        row = pl.multiple_of(c * 8, 8)
        lane = lanes((8, 128))
        both = jnp.where((lane & 4) == 0, turn(got_e[pl.ds(row, 8), :], -4), turn(got_w[pl.ds(row, 8), :], 4))
        ghost = ((lane >= 8) & (lane < 16)) | ((lane >= 32) & (lane < 40))
        for f in range(6):
            field[f, 2, pl.ds(row, 8), :] = jnp.where(ghost, turn(both, -SHIFT[f]), own_seam[f, pl.ds(row, 8), :])
        return carry

    lax.fori_loop(0, 10, seam_halo, 0, unroll=True)

    for c in range(9):
        first(seam, c)
    for c in range(9):
        apply(0, seam, c)
    for c in range(9):
        apply(1, seam, c)
    acc_seam = None
    for c in range(8):
        acc_seam = sums(acc_seam, seam, c)
    lane = lanes((8, 128))
    own_ok = (lane >= 4) & (lane < 124)
    seam_ok = [((lane >= 4 + 24 * m) & (lane < 8 + 24 * m)) | ((lane >= 16 + 24 * m) & (lane < 20 + 24 * m))
               for m in range(2)]
    sub = lax.broadcasted_iota(jnp.int32, (8, 128), 0)
    tables = []
    for m in range(2):
        table = jnp.zeros((8, 128), F32)
        for k in range(6):
            part = jnp.where(own_ok, acc_own[k][m], 0.0) + jnp.where(seam_ok[m], acc_seam[k][0], 0.0)
            table = jnp.where(sub == k, jnp.sum(part, axis=0, keepdims=True), table)
        tables.append(table)
    even = (lane & 1) == 0
    both_m = jnp.where(even, tables[0] + turn(tables[0], -1), tables[1] + turn(tables[1], 1))
    for step in (2, 8, 32):
        both_m = (both_m + turn(both_m, step)) + (turn(both_m, 2 * step) + turn(both_m, 3 * step))
    tile = jnp.sum(jnp.where(lane // 2 == sub, both_m, 0.0), axis=0, keepdims=True)

    def send_tile(s, slots, value):
        slots[places[s]] = value
        for partner in groups[s]:
            pltpu.make_async_remote_copy(
                src_ref=slots.at[places[s]], dst_ref=slots.at[places[s]],
                send_sem=sum_send.at[s], recv_sem=sum_recv.at[s],
                device_id=partner, device_id_type=MESH).start()

    def wait_all(slots, sem):
        rest = slots.at[0:slots.shape[0] - 1]
        pltpu.make_async_copy(rest, rest, sem).wait()

    def take_tiles(s, slots):
        wait_all(slots, sum_recv.at[s])
        terms = [slots[k] for k in range(slots.shape[0])]
        while len(terms) > 1:
            terms = [a + b for a, b in zip(terms[::2], terms[1::2])]
        return terms[0]

    pl.semaphore_wait(word.at[2], 4)
    send_tile(0, tile1, tile)

    def join(c, carry):
        row = pl.multiple_of(8 + c * 8, 8)
        here = pl.ds(row, 8)
        lane = lanes((8, 128))

        def merged(block):
            full = []
            for m in range(2):
                west = turn(block[2], -16 - 24 * m)
                east = turn(block[2], 120 - 24 * m)
                full.append(jnp.where(lane < 4, west, jnp.where(lane >= 124, east, block[m])))
            return full

        wx_c = wx4[:, here, :]
        wy_c = wy4[:, here, :]
        for k in range(3):
            e = basis[k, :, here, :]
            e_n = basis[k, :, pl.ds(row + 1, 8), :]
            for m, value in enumerate(merged(wx_c * (turn(e, -1) - e))):
                dxs[k, m, pl.ds(row - 8, 8), :] = value
            for m, value in enumerate(merged(wy_c * (e_n - e))):
                dys[k, m, pl.ds(row - 8, 8), :] = value
            west_east = merged(e)
            for m in range(2):
                basis[k, m, here, :] = west_east[m]
        for ref, slot in ((ub, 1), (vb, 2)):
            for m, value in enumerate(merged(ref[:, here, :])):
                out[slot, m, pl.ds(row - 8, 8), :] = value
        return carry

    lax.fori_loop(0, 8, join, 0, unroll=2)

    send_tile(1, tile2, take_tiles(0, tile1))
    total = take_tiles(1, tile2)

    m_ = [turn(total, -2 * k) for k in range(6)]
    s_ = [m_[k] + m_[k + 1] for k in range(5)]
    safe = lambda n, d, ok: jnp.where(ok, n / jnp.where(ok, d, 1.0), 0.0)
    ok0 = s_[0] > 0.0
    l10 = safe(s_[1], s_[0], ok0)
    l20 = safe(s_[2], s_[0], ok0)
    d1 = s_[2] - l10 * s_[1]
    e1 = s_[3] - l10 * s_[2]
    ok1 = d1 > 1e-6 * s_[2]
    l21 = safe(e1, d1, ok1)
    d2 = s_[4] - l20 * s_[2] - l21 * e1
    ok2 = ok1 & (d2 > 1e-6 * s_[4])
    y1 = m_[1] - l10 * m_[0]
    y2 = m_[2] - l20 * m_[0] - l21 * y1
    a2 = safe(y2, d2, ok2)
    a1 = safe(y1, d1, ok1) - l21 * a2
    a0 = safe(m_[0], s_[0], ok0) - l10 * a1 - l20 * a2
    coef = [[jnp.broadcast_to(a[:, m:m + 1], (8, 128)) for a in (a0, a1, a2)] for m in range(2)]

    def last(c, carry):
        low = pl.multiple_of(c * 8, 8)
        here = pl.ds(low, 8)
        tall = pl.ds(pl.multiple_of(low + 8, 8), 8)
        for m in range(2):
            k0, k1, k2 = coef[m]
            out[0, m, here, :] = (field[SURF, m, tall, :] + k0 * basis[0, m, tall, :]
                                  + k1 * basis[1, m, tall, :] + k2 * basis[2, m, tall, :])
            out[1, m, here, :] = out[1, m, here, :] - (
                k0 * dxs[0, m, here, :] + k1 * dxs[1, m, here, :] + k2 * dxs[2, m, here, :])
            out[2, m, here, :] = out[2, m, here, :] - (
                k0 * dys[0, m, here, :] + k1 * dys[1, m, here, :] + k2 * dys[2, m, here, :])
        return carry

    lax.fori_loop(0, 8, last, 0, unroll=True)
    for k, (dr, dc) in enumerate(SIDES):
        @pl.when(exists(dr, dc))
        def _():
            halo(k).wait_send()
    for s, slots in enumerate((tile1, tile2)):
        wait_all(slots, sum_send.at[s])


def hand_over(fields, x_o, nu_o, nv_o, sem):
    copies = [pltpu.make_async_copy(fields.at[k], ref, sem.at[k]) for k, ref in enumerate((x_o, nu_o, nv_o))]
    for copy in copies:
        copy.start()
    for copy in copies:
        copy.wait()


def solution(mesh):
    nrow, ncol = mesh.shape["row"], mesh.shape["col"]

    def body(surface, u_face, v_face, bed_depth, wet_mask, rainfall):
        anywhere = pl.BlockSpec(memory_space=pl.ANY)
        vm = lambda *shape: pltpu.VMEM(shape, F32)
        fields = pl.pallas_call(
            functools.partial(kernel, nrow, ncol),
            out_shape=jax.ShapeDtypeStruct((3,) + surface.shape, F32),
            in_specs=[anywhere] * 6,
            out_specs=pl.BlockSpec(memory_space=pltpu.VMEM),
            scratch_shapes=[
                vm(6, 3, TALL, 128),
                pltpu.VMEM((2, ROWS, 128), jnp.int32),
                vm(6, TALL, 128),
                vm(48, 128), vm(48, 128), vm(64, 128),
                vm(48, 128), vm(48, 128), vm(TALL, 128), vm(TALL, 128),
                vm(3, TALL, 128), vm(3, TALL, 128), vm(3, TALL, 128),
                vm(3, TALL, 128), vm(3, TALL, 128), vm(3, TALL, 128), vm(3, TALL, 128),
                vm(3, 3, TALL + 8, 128),
                vm(3, 2, ROWS, 128), vm(3, 2, ROWS, 128),
                vm(nrow, 1, 128), vm(ncol, 1, 128),
                pltpu.SemaphoreType.DMA((7,)),
                pltpu.SemaphoreType.DMA((8,)),
                pltpu.SemaphoreType.DMA((8,)),
                pltpu.SemaphoreType.DMA((2,)),
                pltpu.SemaphoreType.DMA((2,)),
                pltpu.SemaphoreType.REGULAR((3,)),
            ],
            compiler_params=pltpu.CompilerParams(collective_id=0, has_side_effects=True,
                                                 vmem_limit_bytes=8 << 20),
        )(*(pltpu.with_memory_space_constraint(a, pltpu.HBM) for a in (surface, u_face, v_face, bed_depth, wet_mask, rainfall)))
        return pl.pallas_call(
            hand_over,
            out_shape=[jax.ShapeDtypeStruct(surface.shape, F32)] * 3,
            in_specs=[anywhere],
            out_specs=[anywhere] * 3,
            scratch_shapes=[pltpu.SemaphoreType.DMA((3,))],
            compiler_params=pltpu.CompilerParams(vmem_limit_bytes=1 << 20),
        )(fields)

    full = P(None, "row", "col")
    return jax.shard_map(body, mesh=mesh, in_specs=(full, full, full, P("row", "col"), full, full),
                         out_specs=(full, full, full), check_vma=False)
```
